256 devices in a mesh: kv: 4 (over y), blk: 64 (over x, z, core).
Axes of the slice: x: 4, y: 4, z: 8, core: 2. Of those that a mesh axis runs over, the one named last changes fastest.
Arguments:
- hidden: bfloat16 [64, 2560], replicated
- positions: int32 [64], replicated, may hold values from 0 to 16383, as said below
- cache_len: int32 [64], replicated, may hold values from 0 to 16383, as said below
- page_table: int32 [64, 512], replicated, may hold values from -1 to 4095, as said below
- move_dest: int32 [4096, 1], replicated, may hold values from 0 to 63; in each aligned block of 64 rows (0 to 63, 64 to 127, ...) at most 2 rows name the same one
- paged_keys: bfloat16 [4096, 32, 1024], P('blk', None, 'kv')
- paged_values: bfloat16 [4096, 32, 1024], P('blk', None, 'kv'), may hold values from -6 to 6
- qkv_projection: bfloat16 [2560, 4096], P('blk', 'kv'), may hold values from -0.125 to 0.125
- query_norm_gain: float32 [256], replicated, may hold values from 0.5 to 2.5
- key_gain: float32 [256], replicated, may hold values from 0.5 to 2.5
- output_proj: bfloat16 [2048, 2560], P('kv'), may hold values from -0.125 to 0.125
- input_gain: float32 [2560], replicated, may hold values from 0.1 to 1.9
- attn_gain: float32 [2560], replicated, may hold values from 0.1 to 1.9
- ffw_gain: float32 [2560], replicated, may hold values from 0.1 to 1.9
- final_gain: float32 [2560], replicated, may hold values from 0.1 to 1.9
- gate_weight: bfloat16 [2560, 10240], P(None, 'blk'), may hold values from -0.125 to 0.125
- up_weight: bfloat16 [2560, 10240], P(None, 'blk'), may hold values from -0.125 to 0.125
- down_weight: bfloat16 [10240, 2560], P('blk')
Outputs:
- out_hidden: float32 [64, 2560], replicated
- relocated_keys: bfloat16 [8192, 32, 1024], P('blk', None, 'kv')
- relocated_values: bfloat16 [8192, 32, 1024], P('blk', None, 'kv')
The draws below stay inside these ranges and needn't reach their ends.
Inputs may be any that keep to these rules, and one draw needn't show every extreme that they name: `cache_len`: one request holds exactly 16383 tokens. `positions`: at most the request's cache length. `page_table`: entry j of request r is a global slot for j <= cache_len[r] // 32 and -1 after; all slots named are distinct.
All inputs are finite; a program needn't handle non-finite values.
Results may differ from the reference program's by a relative error of at most 0.015.
The reference program's roundings to bfloat16 on the way count: a program that leaves them out, or rounds other values in their place, can miss the bound.
Values may be sent and summed in bfloat16 or wider, within the bound.
No kernel may reach another device: no remote copies, remote signals or barrier semaphores. Data moves between devices by JAX's collectives and lax.ppermute only.
A program may use at most 128 MiB of HBM per device.

```python
import math
import jax
import jax.numpy as jnp
import numpy as np
from jax import lax

MODEL_DIM = 2560
HQ = 8
KEY_HEADS = 4
HEAD_DIM = 256
FF = 10240
QUERY_PER_KV = 2
REQUESTS = 64
PAGE_TOKENS = 32
MAXLEN = 16384
PAGES_PER_SEQ = 512
SLOTS = 64
CAP = 2
SLOTS_BEFORE = 4096
SLOTS_AFTER = 8192
N_BLK = 64


def layout_tables(key):
    key_rank, key_jitter, key_perm, key_shift = jax.random.split(jax.random.fold_in(key, 4711), 4)
    rank = jax.random.permutation(key_rank, REQUESTS).astype(jnp.int32)
    spread = max(REQUESTS // 64, 1)
    ceiling = (MAXLEN - 1) * spread // (spread + rank)
    jitter = jax.random.randint(key_jitter, (REQUESTS,), 0, 1 << 30) % (ceiling + 1)
    lengths = jnp.where(rank == 0, MAXLEN - 1, jitter).astype(jnp.int32)
    pages = lengths // PAGE_TOKENS + 1
    starts = jnp.cumsum(pages) - pages
    column = jnp.arange(PAGES_PER_SEQ, dtype=jnp.int32)
    live = column[None, :] < pages[:, None]
    order = jnp.clip(starts[:, None] + column[None, :], 0, SLOTS_BEFORE - 1)
    shuffle = jax.random.permutation(key_perm, SLOTS_BEFORE).astype(jnp.int32)
    table = jnp.where(live, shuffle[order], -1).astype(jnp.int32)
    shift = jnp.minimum(jax.random.randint(key_shift, (REQUESTS,), 0, 65), lengths)
    shift = jnp.where(rank == 0, 0, shift)
    return (lengths, table, (lengths - shift).astype(jnp.int32))


def draw_cache_len(key, part):
    return layout_tables(key)[0]


def draw_page_table(key, part):
    return layout_tables(key)[1]


def draw_positions(key, part):
    return layout_tables(key)[2]


def draw_hidden(key, part):
    key_start, key_entries, key_cols = jax.random.split(jax.random.fold_in(key, 91), 3)
    start_offset = jax.random.normal(key_start, (REQUESTS, MODEL_DIM), jnp.float32)
    row_scale = jnp.exp(jax.random.uniform(key_entries, (REQUESTS, 1), jnp.float32, 0.0, math.log(10.0))) / 5.0
    col_scale = jnp.exp(jax.random.uniform(key_cols, (1, MODEL_DIM), jnp.float32, -1.15, 1.15))
    return (start_offset * row_scale * col_scale).astype(jnp.bfloat16)


def draw_paged_keys(key, part):
    key_start = jax.random.fold_in(jax.random.fold_in(key, 313), 0)
    start_offset = jax.random.normal(key_start, (SLOTS_BEFORE, PAGE_TOKENS, KEY_HEADS * HEAD_DIM), jnp.float32)
    return start_offset.astype(jnp.bfloat16)


def draw_down_weight(key, part):
    key_base, key_pair = jax.random.split(jax.random.fold_in(key, 577), 2)
    base_entries = jax.random.normal(key_base, (FF, MODEL_DIM), jnp.float32)
    pairing = jax.random.permutation(key_pair, N_BLK).astype(jnp.int32)
    row_block = jnp.arange(FF, dtype=jnp.int32) // (FF // N_BLK)
    col_block = jnp.arange(MODEL_DIM, dtype=jnp.int32) // (MODEL_DIM // N_BLK)
    boost = jnp.where(pairing[row_block][:, None] == col_block[None, :], 16.0, 1.0)
    return (base_entries * boost / math.sqrt(FF)).astype(jnp.bfloat16)


def block_scale(rng, dims, cuts, smallest, largest):
    gain = 1.0
    for dim, blocks in cuts:
        heights = jax.random.uniform(jax.random.fold_in(jax.random.fold_in(rng, 6), dim), (blocks,), jnp.float32, smallest / len(cuts), largest / len(cuts))
        gain = gain * jnp.repeat(jnp.exp(heights), dims[dim] // blocks).reshape((-1,) + (1,) * (len(dims) - 1 - dim))
    return gain


def shared_out(rng, own, number, rows, number_of, top, bound, slope):
    order = jax.random.permutation(rng, number_of)
    crowded, common = load_shares(number_of, rows * top, bound, slope, True), load_shares(number_of, rows * top, bound, slope, False)
    places = jnp.arange(number_of)

    def named(sizes, offset_by):
        used = int((sizes > 0).sum())
        fixed = max(1, used // 4)
        moved = fixed + (places - fixed + offset_by * (used - fixed)) % max(1, number_of - fixed)
        return jnp.zeros((number_of,), jnp.int32).at[order[jnp.where(places < fixed, places, moved)]].set(jnp.asarray(sizes, jnp.int32))

    sizes = jnp.where(number % 4 == 0, named(crowded, number // 4), named(common, number - number // 4 - 1))
    mixed = jax.random.permutation(jax.random.fold_in(own, 3), number_of)
    donor, sink = mixed[0:number_of // 2 * 2:2], mixed[1:number_of // 2 * 2:2]
    margin = jnp.minimum(sizes[donor] - 1, bound - sizes[sink]) // 2
    margin = jnp.where((donor == order[0]) | (sink == order[0]) | (sizes[sink] == 0), 0, jnp.maximum(margin, 0))
    moved = jax.random.randint(jax.random.fold_in(own, 4), (number_of // 2,), 0, 1 << 20) % (margin + 1)
    sizes = sizes.at[donor].add(-moved).at[sink].add(moved)
    items = jnp.searchsorted(jnp.cumsum(sizes), jnp.arange(rows * top), side="right").astype(jnp.int32)
    table = items.reshape(top, rows).T
    table = table[jax.random.permutation(jax.random.fold_in(own, 1), rows)]
    offset_by = jax.random.randint(jax.random.fold_in(own, 2), (rows, 1), 0, top)
    return jnp.take_along_axis(table, (jnp.arange(top)[None, :] + offset_by) % top, axis=1)


def load_shares(count, total, reach, lean, full):
    loads = [(1 << 20) // math.isqrt(rank ** lean) + 1 for rank in range(1, count + 1)]
    largest = reach if full else min(reach, max(-(-total // count), total * loads[0] // sum(loads)))
    least = 1 if total - largest >= count - 1 else 0
    given, spare = [largest] + [least] * (count - 1), total - largest - least * (count - 1)
    while spare > 0:
        candidates = [i for i in range(1, count) if given[i] < largest] or [i for i in range(1, count) if given[i] < reach]
        whole, remaining = sum([loads[i] for i in candidates]), spare
        for i in candidates:
            more = min(reach - given[i], max(1, remaining * loads[i] // whole), spare)
            given[i] = given[i] + more
            spare = spare - more
    return np.array(given)


def scatter_about(stream_key, extent, scale, reach, shards=(), held_as=jnp.bfloat16):
    values = scale * jax.random.normal(stream_key, extent, jnp.float32)
    if shards:
        values = values * block_scale(stream_key, extent, shards, -0.22, 0.18)
    return jnp.clip(values, -reach, reach).astype(held_as)


def setup_inputs(seed: int = 0) -> dict:
    keys = jax.random.split(jax.random.key(seed), 19)
    hidden = draw_hidden(jax.random.fold_in(keys[18], 71), 0)
    positions = draw_positions(jax.random.fold_in(keys[18], 71), 0)
    cache_len = draw_cache_len(jax.random.fold_in(keys[18], 71), 0)
    page_table = draw_page_table(jax.random.fold_in(keys[18], 71), 0)
    move_dest_keys = jax.random.split(jax.random.fold_in(keys[4], 1), SLOTS_BEFORE // SLOTS)
    move_dest_turns = jax.random.permutation(jax.random.fold_in(keys[4], 3), SLOTS_BEFORE // SLOTS)
    move_dest = jax.vmap(lambda own, number: shared_out(jax.random.fold_in(keys[4], 2), own, number, SLOTS, N_BLK, 1, CAP, 2))(move_dest_keys, move_dest_turns).reshape((SLOTS_BEFORE, 1))
    paged_keys = draw_paged_keys(jax.random.fold_in(keys[18], 71), 0)
    paged_values = scatter_about(keys[6], (SLOTS_BEFORE, PAGE_TOKENS, KEY_HEADS * HEAD_DIM), 1.0, 6.0, ((0, 64), (2, 4)))
    qkv_projection = scatter_about(keys[7], (MODEL_DIM, KEY_HEADS * (QUERY_PER_KV + 2) * HEAD_DIM), MODEL_DIM ** -0.5, 0.125, ((0, 64), (1, 4)))
    query_norm_gain = jnp.clip(jnp.exp(jax.random.uniform(keys[8], (HEAD_DIM,), jnp.float32, math.log(0.5), math.log(2.5))), 0.5, 2.5)
    key_gain = jnp.clip(jnp.exp(jax.random.uniform(keys[9], (HEAD_DIM,), jnp.float32, math.log(0.5), math.log(2.5))), 0.5, 2.5)
    output_proj = scatter_about(keys[10], (HQ * HEAD_DIM, MODEL_DIM), (HQ * HEAD_DIM) ** -0.5, 0.125, ((0, 4),))
    input_gain = jnp.clip(1.0 + 0.18 * jax.random.normal(keys[11], (MODEL_DIM,), jnp.float32), 0.1, 1.9)
    attn_gain = jnp.clip(1.0 + 0.18 * jax.random.normal(keys[12], (MODEL_DIM,), jnp.float32), 0.1, 1.9)
    ffw_gain = jnp.clip(1.0 + 0.18 * jax.random.normal(keys[13], (MODEL_DIM,), jnp.float32), 0.1, 1.9)
    final_gain = jnp.clip(1.0 + 0.18 * jax.random.normal(keys[14], (MODEL_DIM,), jnp.float32), 0.1, 1.9)
    gate_weight = scatter_about(keys[15], (MODEL_DIM, FF), MODEL_DIM ** -0.5, 0.125, ((1, 64),))
    up_weight = scatter_about(keys[16], (MODEL_DIM, FF), MODEL_DIM ** -0.5, 0.125, ((1, 64),))
    down_weight = draw_down_weight(jax.random.fold_in(keys[18], 71), 0)
    return dict(hidden=hidden, positions=positions, cache_len=cache_len, page_table=page_table, move_dest=move_dest, paged_keys=paged_keys, paged_values=paged_values, qkv_projection=qkv_projection, query_norm_gain=query_norm_gain, key_gain=key_gain, output_proj=output_proj, input_gain=input_gain, attn_gain=attn_gain, ffw_gain=ffw_gain, final_gain=final_gain, gate_weight=gate_weight, up_weight=up_weight, down_weight=down_weight)


EPSILON = 1e-06
QK_SCALE = 0.0625
ROPE_LOG = math.log(1000000.0)
NEG_LARGE = -1e+30

def root_mean_norm(values, scale_vec):
    return values * lax.rsqrt(lax.optimization_barrier(jnp.mean(values * values, axis=-1, keepdims=True)) + EPSILON) * scale_vec

def rotary_embed(values, positions):
    head_width = values.shape[-1]
    half_width = head_width // 2
    frequency = jnp.exp(-(2.0 * jnp.arange(half_width, dtype=jnp.float32) / head_width) * ROPE_LOG)
    angles = positions.astype(jnp.float32)[:, None] * frequency[None, :]
    cosine = jnp.cos(angles)[:, None, :]
    sine_part = jnp.sin(angles)[:, None, :]
    front = values[..., :half_width]
    back = values[..., half_width:]
    return jnp.concatenate([front * cosine - back * sine_part, back * cosine + front * sine_part], axis=-1)

def reference(hidden, positions, cache_len, page_table, move_dest, paged_keys, paged_values, qkv_projection, query_norm_gain, key_gain, output_proj, input_gain, attn_gain, ffw_gain, final_gain, gate_weight, up_weight, down_weight):
    request_count = hidden.shape[0]
    normed = root_mean_norm(hidden.astype(jnp.float32), input_gain).astype(jnp.bfloat16)
    projected_input = jnp.dot(normed, qkv_projection, preferred_element_type=jnp.float32).astype(jnp.bfloat16)
    projected_input = projected_input.reshape(request_count, KEY_HEADS, QUERY_PER_KV + 2, HEAD_DIM).astype(jnp.float32)
    query_head_rows = root_mean_norm(projected_input[:, :, :QUERY_PER_KV], query_norm_gain).reshape(request_count, KEY_HEADS * QUERY_PER_KV, HEAD_DIM)
    query_vectors = rotary_embed(query_head_rows, positions).astype(jnp.bfloat16).reshape(request_count, KEY_HEADS, QUERY_PER_KV, HEAD_DIM)
    fresh_keys = rotary_embed(root_mean_norm(projected_input[:, :, QUERY_PER_KV], key_gain), positions).astype(jnp.bfloat16)
    fresh_values = projected_input[:, :, QUERY_PER_KV + 1].astype(jnp.bfloat16)
    requests = jnp.arange(request_count, dtype=jnp.int32)
    target_slot = page_table[requests, (cache_len // PAGE_TOKENS).astype(jnp.int32)]
    position_offsets = (cache_len % PAGE_TOKENS).astype(jnp.int32)
    updated_keys = paged_keys.at[target_slot, position_offsets].set(fresh_keys.reshape(request_count, KEY_HEADS * HEAD_DIM))
    updated_values = paged_values.at[target_slot, position_offsets].set(fresh_values.reshape(request_count, KEY_HEADS * HEAD_DIM))

    def attend_one(request):
        page_table_row = jnp.maximum(page_table[request], 0)
        key_entries = updated_keys[page_table_row].reshape(PAGES_PER_SEQ * PAGE_TOKENS, KEY_HEADS, HEAD_DIM).astype(jnp.float32)
        value_entries = updated_values[page_table_row].reshape(PAGES_PER_SEQ * PAGE_TOKENS, KEY_HEADS, HEAD_DIM).astype(jnp.float32)
        key_valid = jnp.arange(PAGES_PER_SEQ * PAGE_TOKENS, dtype=jnp.int32) <= cache_len[request]
        scores = jnp.einsum('hgd,thd->hgt', query_vectors[request].astype(jnp.float32), key_entries) * QK_SCALE
        scores = jnp.where(key_valid, scores, NEG_LARGE)
        top_score = lax.optimization_barrier(jnp.max(scores, axis=-1, keepdims=True))
        weights = jnp.where(key_valid, jnp.exp(scores - top_score), 0.0)
        denom_sum = lax.optimization_barrier(jnp.sum(weights, axis=-1))
        rounded = lax.optimization_barrier(weights.astype(jnp.bfloat16))
        mixture = jnp.einsum('hgt,thd->hgd', rounded.astype(jnp.float32), value_entries)
        return (mixture / denom_sum[..., None]).reshape(HQ * HEAD_DIM)
    attended = lax.map(attend_one, requests).astype(jnp.bfloat16)
    attn_out = jnp.dot(attended, output_proj, preferred_element_type=jnp.float32)
    residual = hidden.astype(jnp.float32) + root_mean_norm(attn_out, attn_gain)
    ffw_in = root_mean_norm(residual, ffw_gain).astype(jnp.bfloat16)
    gate_proj = jnp.dot(ffw_in, gate_weight, preferred_element_type=jnp.float32)
    up_proj = jnp.dot(ffw_in, up_weight, preferred_element_type=jnp.float32)
    hidden_units = (jax.nn.gelu(gate_proj, approximate=True) * up_proj).astype(jnp.bfloat16)
    ffw_out = jnp.dot(hidden_units, down_weight, preferred_element_type=jnp.float32)
    out_hidden = residual + root_mean_norm(ffw_out, final_gain)
    destination = move_dest[:, 0].astype(jnp.int32)
    dest_onehot = (destination[:, None] == jnp.arange(N_BLK, dtype=jnp.int32)[None, :]).astype(jnp.int32)
    dest_onehot = dest_onehot.reshape(N_BLK, SLOTS, N_BLK)
    slot_rank = lax.optimization_barrier(jnp.sum((jnp.cumsum(dest_onehot, axis=1) - dest_onehot) * dest_onehot, axis=-1)).reshape(SLOTS_BEFORE)
    source = jnp.arange(SLOTS_BEFORE, dtype=jnp.int32) // SLOTS
    fresh_index = (destination * (N_BLK * CAP) + source * CAP + slot_rank).astype(jnp.int32)
    relocated_keys = jnp.zeros((SLOTS_AFTER, PAGE_TOKENS, KEY_HEADS * HEAD_DIM), jnp.bfloat16).at[fresh_index].set(updated_keys)
    relocated_values = jnp.zeros((SLOTS_AFTER, PAGE_TOKENS, KEY_HEADS * HEAD_DIM), jnp.bfloat16).at[fresh_index].set(updated_values)
    return (out_hidden, relocated_keys, relocated_values)
```

```python
import functools
import math

import jax
import jax.numpy as jnp
from jax import lax
from jax.experimental import pallas as pl
from jax.experimental.pallas import tpu as pltpu
from jax.sharding import PartitionSpec as P

EPSILON = 1e-06
QK_SCALE = 0.0625
ROPE_LOG = math.log(1000000.0)
NEG_LARGE = -1e30
LANES = 128
BF16 = jnp.bfloat16
F32 = jnp.float32


def call(body, out_shape, n_in, flops, bytes_accessed):
    vmem = pl.BlockSpec(memory_space=pltpu.VMEM)
    return pl.pallas_call(
        body,
        out_shape=out_shape,
        in_specs=[vmem] * n_in,
        out_specs=jax.tree.map(lambda _: vmem, out_shape),
        cost_estimate=pl.CostEstimate(
            flops=flops, bytes_accessed=bytes_accessed, transcendentals=0
        ),
    )


def exchange(x):
    return lax.all_to_all(x, "blk", split_axis=0, concat_axis=0, tiled=True)


def inv_rms(square_sum, width):
    return lax.rsqrt(square_sum / width + EPSILON)


def tile_sum(x):
    return jnp.sum(jnp.sum(x, axis=1, keepdims=True), axis=0, keepdims=True)


def head_body(terms_ref, cos_ref, sin_ref, qgain_ref, kgain_ref, all_ref, own_ref):
    total = jnp.sum(terms_ref[...].astype(F32), axis=0)
    total = total.astype(BF16).astype(F32)
    cosine, sine = cos_ref[...], sin_ref[...]
    rows = []
    heads = total.shape[0] // 2 - 1
    for h in range(heads):
        gain = qgain_ref[...] if h < heads - 1 else kgain_ref[...]
        pair = total[2 * h : 2 * h + 2]
        pair = pair * inv_rms(tile_sum(pair * pair), 2 * LANES) * gain
        front, back = pair[0:1], pair[1:2]
        rows.append(front * cosine - back * sine)
        rows.append(back * cosine + front * sine)
    rows.append(total[2 * heads :])
    done = jnp.concatenate(rows, axis=0).astype(BF16)
    own_ref[...] = done
    all_ref[...] = jnp.broadcast_to(done[None], all_ref.shape)


def split3(x):
    first = x.astype(BF16).astype(F32)
    second = (x - first).astype(BF16).astype(F32)
    return first, second, x - first - second


def attend_body(groups, query_ref, keys_ref, values_ref, limit_ref, out_ref):
    slots, page, width = keys_ref.shape
    requests = query_ref.shape[0]
    tokens = slots * page
    keys = keys_ref[...].reshape(tokens, width)
    values = values_ref[...].reshape(tokens, width)
    spread = (
        lax.broadcasted_iota(jnp.int32, (slots, tokens), 1) // page
        == lax.broadcasted_iota(jnp.int32, (slots, tokens), 0)
    ).astype(F32).astype(BF16)
    limit = jnp.dot(limit_ref[...], spread, preferred_element_type=F32)
    offset = (lax.broadcasted_iota(jnp.int32, (requests, tokens), 1) % page).astype(F32)
    valid = offset < limit
    lane = lax.broadcasted_iota(jnp.int32, (requests, LANES), 1)
    extra = jnp.zeros((requests, LANES), F32)
    for g in range(groups):
        scores = lax.dot_general(
            query_ref[:, g * width : (g + 1) * width],
            keys,
            (((1,), (1,)), ((), ())),
            preferred_element_type=F32,
        )
        scores = jnp.where(valid, scores * QK_SCALE, NEG_LARGE)
        peak = jnp.max(scores, axis=1, keepdims=True)
        weights = jnp.where(valid, jnp.exp(scores - peak), 0.0)
        total = jnp.sum(weights, axis=1, keepdims=True)
        mixed = jnp.dot(weights.astype(BF16), values, preferred_element_type=F32)
        out_ref[:, g * width : (g + 1) * width] = mixed.astype(BF16)
        for i, part in enumerate(split3(peak) + split3(total)):
            extra = jnp.where(lane == 8 * g + i, part, extra)
    start = groups * width
    out_ref[:, start : start + LANES] = extra.astype(BF16)
    rest = out_ref.shape[1] - start - LANES
    out_ref[:, start + LANES :] = jnp.zeros((requests, rest), BF16)


def merge_body(groups, parts_ref, own_ref, proj_ref, out_ref):
    own = own_ref[...].astype(F32)
    rows = []
    stats = parts_ref[:, 2 * groups : 2 * groups + 1, :].astype(F32)
    key = own[2 * groups : 2 * groups + 2]
    value = own[2 * groups + 2 : 2 * groups + 4]
    for g in range(groups):
        def stat(i):
            at = 8 * g + i
            return stats[:, :, at : at + 1]

        peaks = stat(0) + stat(1) + stat(2)
        sums = stat(3) + stat(4) + stat(5)
        fresh = tile_sum(own[2 * g : 2 * g + 2] * key)[None] * QK_SCALE
        peak = jnp.maximum(jnp.max(peaks, axis=0, keepdims=True), fresh)
        scale = jnp.exp(peaks - peak)
        fresh = jnp.exp(fresh - peak)
        total = jnp.sum(scale * sums, axis=0) + fresh[0]
        mixed = jnp.sum(scale * parts_ref[:, 2 * g : 2 * g + 2, :].astype(F32), axis=0)
        mixed = mixed + fresh[0].astype(BF16).astype(F32) * value
        rows.append(mixed / total)
    heads = jnp.concatenate(rows, axis=0)
    flat = jnp.concatenate([heads[i : i + 1] for i in range(heads.shape[0])], axis=1)
    flat = jnp.broadcast_to(flat, (8, flat.shape[1])).astype(BF16)
    terms = jnp.dot(flat, proj_ref[...], preferred_element_type=F32)
    out_ref[...] = jnp.concatenate(
        [terms[0:1, i * LANES : (i + 1) * LANES] for i in range(out_ref.shape[0])], axis=0
    )


def residual_body(*refs):
    part_refs = refs[:-5]
    hidden_ref, attn_gain_ref, ffw_gain_ref, residual_ref, all_ref = refs[-5:]
    parts = [ref[...] for ref in part_refs]
    while len(parts) > 1:
        half = len(parts) // 2
        parts = [parts[i] + parts[i + half] for i in range(half)]
    attn = parts[0]
    width = attn.shape[0] * attn.shape[1]
    residual = (
        hidden_ref[...].astype(F32)
        + attn * inv_rms(tile_sum(attn * attn), width) * attn_gain_ref[...]
    )
    residual_ref[...] = residual
    ffw_in = residual * inv_rms(tile_sum(residual * residual), width) * ffw_gain_ref[...]
    all_ref[...] = jnp.broadcast_to(ffw_in.astype(BF16)[None], all_ref.shape)


def ffw_body(x_ref, gate_ref, up_ref, down_ref, out_ref):
    x = x_ref[...]
    gate = jnp.dot(x, gate_ref[...], preferred_element_type=F32)
    up = jnp.dot(x, up_ref[...], preferred_element_type=F32)
    units = (jax.nn.gelu(gate, approximate=True) * up).astype(BF16)
    out_ref[...] = jnp.dot(units, down_ref[...], preferred_element_type=F32).astype(BF16)


def output_body(terms_ref, residual_ref, gain_ref, all_ref):
    total = jnp.sum(terms_ref[...].astype(F32), axis=0)
    width = total.shape[0] * total.shape[1]
    row = residual_ref[...] + total * inv_rms(tile_sum(total * total), width) * gain_ref[...]
    all_ref[...] = jnp.broadcast_to(row.astype(BF16)[None], all_ref.shape)


def migrate(pages, source_of, blocks, capacity):
    send = jnp.take(pages, source_of, axis=0, mode="fill", fill_value=0)
    send = send.reshape((blocks, capacity) + pages.shape[1:])
    got = lax.all_to_all(send, "blk", split_axis=0, concat_axis=0, tiled=True)
    return got.reshape((blocks * capacity,) + pages.shape[1:])


def patch(pages, flat_pos, rows):
    count, page, width = pages.shape
    flat = pages.reshape(count * page, width).at[flat_pos].set(rows, mode="drop")
    return flat.reshape(count, page, width)


def local(
    hidden,
    positions,
    cache_len,
    page_table,
    move_dest,
    paged_keys,
    paged_values,
    qkv_projection,
    query_norm_gain,
    key_gain,
    output_proj,
    input_gain,
    attn_gain,
    ffw_gain,
    final_gain,
    gate_weight,
    up_weight,
    down_weight,
):
    blocks = lax.axis_size("blk")
    kv_size = lax.axis_size("kv")
    device = lax.axis_index("blk")
    requests, model = hidden.shape
    head = query_norm_gain.shape[0]
    slots, page, _ = paged_keys.shape
    pages_per_seq = page_table.shape[1]
    capacity = max(2, (slots + blocks - 1) // blocks)
    recv_slots = blocks * capacity
    feature_rows, columns = qkv_projection.shape
    groups = columns // head - 2
    col_tiles = columns // LANES
    model_tiles = model // LANES
    assert requests == blocks

    hidden32 = hidden.astype(F32)
    scale = lax.rsqrt(jnp.mean(hidden32 * hidden32, axis=-1, keepdims=True) + EPSILON)
    start = device * feature_rows
    normed = (
        lax.dynamic_slice_in_dim(hidden, start, feature_rows, 1).astype(F32)
        * scale
        * lax.dynamic_slice_in_dim(input_gain, start, feature_rows, 0)
    ).astype(BF16)
    terms = jnp.dot(normed, qkv_projection, preferred_element_type=F32).astype(BF16)
    terms = exchange(terms.reshape(requests, col_tiles, LANES))

    frequency = jnp.exp(-(2.0 * jnp.arange(head // 2, dtype=F32) / head) * ROPE_LOG)
    position = lax.dynamic_slice_in_dim(positions, device, 1).astype(F32)
    angles = position[:, None] * frequency[None, :]
    tile = (head // LANES, LANES)
    every, own = call(
        head_body,
        (
            jax.ShapeDtypeStruct((requests, col_tiles, LANES), BF16),
            jax.ShapeDtypeStruct((col_tiles, LANES), BF16),
        ),
        5,
        requests * columns,
        4 * requests * columns,
    )(
        terms,
        jnp.cos(angles),
        jnp.sin(angles),
        query_norm_gain.reshape(tile),
        key_gain.reshape(tile),
    )
    every = exchange(every).reshape(requests, columns)

    slot_ids = device * slots + jnp.arange(slots, dtype=jnp.int32)
    page_starts = jnp.arange(pages_per_seq, dtype=jnp.int32) * page
    held = jnp.clip(cache_len[:, None] - page_starts[None, :], 0, page)
    limit = jnp.sum(
        jnp.where(page_table[:, None, :] == slot_ids[None, :, None], held[:, None, :], 0), axis=-1
    ).astype(BF16)
    parts = call(
        functools.partial(attend_body, groups),
        jax.ShapeDtypeStruct((requests, columns), BF16),
        4,
        4 * groups * requests * slots * page * head,
        4 * slots * page * head,
    )(every, paged_keys, paged_values, limit)
    parts = exchange(parts.reshape(requests, col_tiles, LANES))
    attn_terms = call(
        functools.partial(merge_body, groups),
        jax.ShapeDtypeStruct((model_tiles, LANES), F32),
        3,
        16 * groups * head * model,
        2 * groups * head * model,
    )(parts, own, output_proj)

    everyone = [attn_terms] + [
        lax.ppermute(attn_terms, "kv", [(i, (i + d) % kv_size) for i in range(kv_size)])
        for d in range(1, kv_size)
    ]
    wide = (model_tiles, LANES)
    residual, ffw_in = call(
        residual_body,
        (
            jax.ShapeDtypeStruct(wide, F32),
            jax.ShapeDtypeStruct((requests,) + wide, BF16),
        ),
        kv_size + 3,
        model * 16,
        2 * requests * model,
    )(
        *everyone,
        lax.dynamic_slice_in_dim(hidden, device, 1, 0).reshape(wide),
        attn_gain.reshape(wide),
        ffw_gain.reshape(wide),
    )
    ffw_in = exchange(ffw_in).reshape(requests, model)
    units = gate_weight.shape[1]
    ffw_terms = call(
        ffw_body,
        jax.ShapeDtypeStruct((requests, model), BF16),
        4,
        6 * requests * units * model,
        6 * units * model,
    )(ffw_in, gate_weight, up_weight, down_weight)
    ffw_terms = exchange(ffw_terms.reshape((requests,) + wide))
    out_rows = call(
        output_body,
        jax.ShapeDtypeStruct((requests,) + wide, BF16),
        3,
        requests * model,
        4 * requests * model,
    )(ffw_terms, residual, final_gain.reshape(wide))
    out_hidden = exchange(out_rows).reshape(requests, model).astype(F32)

    dest = lax.dynamic_slice_in_dim(move_dest[:, 0], device * slots, slots)
    slot_iota = jnp.arange(slots, dtype=jnp.int32)
    earlier = (dest[None, :] == dest[:, None]) & (slot_iota[None, :] < slot_iota[:, None])
    outgoing = dest * capacity + jnp.sum(earlier.astype(jnp.int32), axis=1)
    match = outgoing[None, :] == jnp.arange(recv_slots, dtype=jnp.int32)[:, None]
    source_of = slots + jnp.sum(jnp.where(match, slot_iota[None, :] - slots, 0), axis=1)
    relocated_keys = migrate(paged_keys, source_of, blocks, capacity)
    relocated_values = migrate(paged_values, source_of, blocks, capacity)

    target = jnp.sum(
        jnp.where(
            jnp.arange(pages_per_seq, dtype=jnp.int32)[None, :] == cache_len[:, None] // page,
            page_table,
            0,
        ),
        axis=1,
    )
    all_dest = move_dest[:, 0]
    all_slots = jnp.arange(all_dest.shape[0], dtype=jnp.int32)
    target_dest = jnp.sum(
        jnp.where(all_slots[None, :] == target[:, None], all_dest[None, :], 0), axis=1
    )
    target_rank = jnp.sum(
        (
            (all_slots[None, :] // slots == target[:, None] // slots)
            & (all_slots[None, :] < target[:, None])
            & (all_dest[None, :] == target_dest[:, None])
        ).astype(jnp.int32),
        axis=1,
    )
    arrival = target // slots * capacity + target_rank
    flat_pos = jnp.where(
        target_dest == device, arrival * page + cache_len % page, recv_slots * page
    )
    fresh_keys = every[:, groups * head : (groups + 1) * head]
    fresh_values = every[:, (groups + 1) * head :]
    relocated_keys = patch(relocated_keys, flat_pos, fresh_keys)
    relocated_values = patch(relocated_values, flat_pos, fresh_values)
    return (out_hidden, relocated_keys, relocated_values)


def solution(mesh):
    return jax.shard_map(
        local,
        mesh=mesh,
        in_specs=(
            P(),
            P(),
            P(),
            P(),
            P(),
            P("blk", None, "kv"),
            P("blk", None, "kv"),
            P("blk", "kv"),
            P(),
            P(),
            P("kv", None),
            P(),
            P(),
            P(),
            P(),
            P(None, "blk"),
            P(None, "blk"),
            P("blk", None),
        ),
        out_specs=(P(), P("blk", None, "kv"), P("blk", None, "kv")),
        check_vma=False,
    )
```

```python
import functools
import math

import jax
import jax.numpy as jnp
from jax import lax
from jax.experimental import pallas as pl
from jax.experimental.pallas import tpu as pltpu
from jax.sharding import PartitionSpec as P

EPSILON = 1e-06
QK_SCALE = 0.0625
ROPE_LOG = math.log(1000000.0)
NEG_LARGE = -1e30
LANES = 128
BF16 = jnp.bfloat16
F32 = jnp.float32


def call(body, out_shape, n_in, flops, bytes_accessed):
    vmem = pl.BlockSpec(memory_space=pltpu.VMEM)
    return pl.pallas_call(
        body,
        out_shape=out_shape,
        in_specs=[vmem] * n_in,
        out_specs=jax.tree.map(lambda _: vmem, out_shape),
        cost_estimate=pl.CostEstimate(
            flops=flops, bytes_accessed=bytes_accessed, transcendentals=0
        ),
    )


def tie(*values):
    return lax.optimization_barrier(values)


def exchange(x):
    return lax.all_to_all(x, "blk", split_axis=0, concat_axis=0, tiled=True)


def inv_rms(square_sum, width):
    return lax.rsqrt(square_sum / width + EPSILON)


def tile_sum(x):
    return jnp.sum(jnp.sum(x, axis=1, keepdims=True), axis=0, keepdims=True)


def head_body(terms_ref, cos_ref, sin_ref, qgain_ref, kgain_ref, all_ref, own_ref):
    total = jnp.sum(terms_ref[...].astype(F32), axis=0)
    total = total.astype(BF16).astype(F32)
    cosine, sine = cos_ref[...], sin_ref[...]
    rows = []
    heads = total.shape[0] // 2 - 1
    for h in range(heads):
        gain = qgain_ref[...] if h < heads - 1 else kgain_ref[...]
        pair = total[2 * h : 2 * h + 2]
        pair = pair * inv_rms(tile_sum(pair * pair), 2 * LANES) * gain
        front, back = pair[0:1], pair[1:2]
        rows.append(front * cosine - back * sine)
        rows.append(back * cosine + front * sine)
    rows.append(total[2 * heads :])
    done = jnp.concatenate(rows, axis=0).astype(BF16)
    own_ref[...] = done
    all_ref[...] = jnp.broadcast_to(done[None], all_ref.shape)


def split3(x):
    first = x.astype(BF16).astype(F32)
    second = (x - first).astype(BF16).astype(F32)
    return first, second, x - first - second


def attend_body(groups, query_ref, keys_ref, values_ref, limit_ref, out_ref):
    slots, page, width = keys_ref.shape
    requests = query_ref.shape[0]
    tokens = slots * page
    keys = keys_ref[...].reshape(tokens, width)
    values = values_ref[...].reshape(tokens, width)
    spread = (
        lax.broadcasted_iota(jnp.int32, (slots, tokens), 1) // page
        == lax.broadcasted_iota(jnp.int32, (slots, tokens), 0)
    ).astype(F32).astype(BF16)
    limit = jnp.dot(limit_ref[...], spread, preferred_element_type=F32)
    offset = (lax.broadcasted_iota(jnp.int32, (requests, tokens), 1) % page).astype(F32)
    valid = offset < limit
    lane = lax.broadcasted_iota(jnp.int32, (requests, LANES), 1)
    extra = jnp.zeros((requests, LANES), F32)
    for g in range(groups):
        scores = lax.dot_general(
            query_ref[:, g * width : (g + 1) * width],
            keys,
            (((1,), (1,)), ((), ())),
            preferred_element_type=F32,
        )
        scores = jnp.where(valid, scores * QK_SCALE, NEG_LARGE)
        peak = jnp.max(scores, axis=1, keepdims=True)
        weights = jnp.where(valid, jnp.exp(scores - peak), 0.0)
        total = jnp.sum(weights, axis=1, keepdims=True)
        mixed = jnp.dot(weights.astype(BF16), values, preferred_element_type=F32)
        out_ref[:, g * width : (g + 1) * width] = mixed.astype(BF16)
        for i, part in enumerate(split3(peak) + split3(total)):
            extra = jnp.where(lane == 8 * g + i, part, extra)
    start = groups * width
    out_ref[:, start : start + LANES] = extra.astype(BF16)
    rest = out_ref.shape[1] - start - LANES
    out_ref[:, start + LANES :] = jnp.zeros((requests, rest), BF16)


def merge_body(groups, parts_ref, own_ref, proj_ref, out_ref):
    own = own_ref[...].astype(F32)
    rows = []
    stats = parts_ref[:, 2 * groups : 2 * groups + 1, :].astype(F32)
    key = own[2 * groups : 2 * groups + 2]
    value = own[2 * groups + 2 : 2 * groups + 4]
    for g in range(groups):
        def stat(i):
            at = 8 * g + i
            return stats[:, :, at : at + 1]

        peaks = stat(0) + stat(1) + stat(2)
        sums = stat(3) + stat(4) + stat(5)
        fresh = tile_sum(own[2 * g : 2 * g + 2] * key)[None] * QK_SCALE
        peak = jnp.maximum(jnp.max(peaks, axis=0, keepdims=True), fresh)
        scale = jnp.exp(peaks - peak)
        fresh = jnp.exp(fresh - peak)
        total = jnp.sum(scale * sums, axis=0) + fresh[0]
        mixed = jnp.sum(scale * parts_ref[:, 2 * g : 2 * g + 2, :].astype(F32), axis=0)
        mixed = mixed + fresh[0].astype(BF16).astype(F32) * value
        rows.append(mixed / total)
    heads = jnp.concatenate(rows, axis=0)
    flat = jnp.concatenate([heads[i : i + 1] for i in range(heads.shape[0])], axis=1)
    flat = jnp.broadcast_to(flat, (8, flat.shape[1])).astype(BF16)
    terms = jnp.dot(flat, proj_ref[...], preferred_element_type=F32)
    tile = jnp.concatenate(
        [terms[0:1, i * LANES : (i + 1) * LANES] for i in range(out_ref.shape[1])], axis=0
    )
    out_ref[...] = jnp.broadcast_to(tile[None], out_ref.shape)


def residual_body(
    parts_ref, hidden_ref, attn_gain_ref, ffw_gain_ref, residual_ref, all_ref
):
    attn = jnp.sum(parts_ref[...], axis=0)
    width = attn.shape[0] * attn.shape[1]
    residual = (
        hidden_ref[...].astype(F32)
        + attn * inv_rms(tile_sum(attn * attn), width) * attn_gain_ref[...]
    )
    residual_ref[...] = residual
    ffw_in = residual * inv_rms(tile_sum(residual * residual), width) * ffw_gain_ref[...]
    all_ref[...] = jnp.broadcast_to(ffw_in.astype(BF16)[None], all_ref.shape)


def ffw_body(x_ref, gate_ref, up_ref, down_ref, out_ref):
    x = x_ref[...]
    gate = jnp.dot(x, gate_ref[...], preferred_element_type=F32)
    up = jnp.dot(x, up_ref[...], preferred_element_type=F32)
    units = (jax.nn.gelu(gate, approximate=True) * up).astype(BF16)
    out_ref[...] = jnp.dot(units, down_ref[...], preferred_element_type=F32).astype(BF16)


def output_body(terms_ref, residual_ref, gain_ref, all_ref):
    total = jnp.sum(terms_ref[...].astype(F32), axis=0)
    width = total.shape[0] * total.shape[1]
    row = residual_ref[...] + total * inv_rms(tile_sum(total * total), width) * gain_ref[...]
    all_ref[...] = jnp.broadcast_to(row.astype(BF16)[None], all_ref.shape)


def gather_body(source_ref, pages_ref, *outs):
    per = outs[0].shape[0]
    slots = pages_ref.shape[0]
    for j, out in enumerate(outs):

        @pl.loop(0, per, unroll=4)
        def _(q, j=j, out=out):
            source = source_ref[j * per + q]
            page = pages_ref[jnp.minimum(source, slots - 1)]
            out[q] = jnp.where(source < slots, page, jnp.zeros_like(page))


def regroup_body(count, *refs):
    ins, outs, sem = refs[:count], refs[count:-1], refs[-1]
    cap = outs[0].shape[0] // count
    for j, out in enumerate(outs):
        for i, chunk in enumerate(ins):
            pltpu.make_async_copy(
                chunk.at[j * cap : (j + 1) * cap], out.at[i * cap : (i + 1) * cap], sem.at[j]
            ).start()
    for j, out in enumerate(outs):
        pltpu.make_async_copy(out, out, sem.at[j]).wait()


def assemble_body(counts, cap, place_ref, arrive_ref, fresh_ref, *refs):
    arrays = len(counts)
    chunks, outs = refs[: sum(counts)], refs[sum(counts) : -3]
    pages, copy_sem, patch_sem = refs[-3:]
    page = outs[0].shape[1]
    requests, tiles = fresh_ref.shape[:2]
    first = 0
    for p, out in enumerate(outs):
        inner = chunks[first].shape[0] // cap
        for j in range(counts[p]):
            for i in range(inner):
                at = place_ref[p, j * inner + i] * cap
                pltpu.make_async_copy(
                    chunks[first + j].at[i * cap : (i + 1) * cap],
                    out.at[pl.ds(at, cap)],
                    copy_sem.at[p],
                ).start()
        first += counts[p]
    for p, out in enumerate(outs):
        pltpu.make_async_copy(out, out, copy_sem.at[p]).wait()

    def each(act):
        @pl.loop(0, requests)
        def _(r):
            where = arrive_ref[r]

            @pl.when(where >= 0)
            def _():
                for p, out in enumerate(outs):
                    act(p, r, out.at[where // page], where % page)

    def fetch(p, r, slot):
        return pltpu.make_async_copy(slot, pages.at[p, r], patch_sem.at[p, r])

    def put(p, r, slot):
        return pltpu.make_async_copy(pages.at[p, r], slot, patch_sem.at[p, r])

    def change(p, r, slot, offset):
        fetch(p, r, slot).wait()
        at = tiles - 2 * arrays + 2 * p
        new = fresh_ref[r].astype(F32)
        row = jnp.concatenate([new[at : at + 1], new[at + 1 : at + 2]], axis=1)
        old = pages[p, r].astype(F32)
        here = lax.broadcasted_iota(jnp.int32, old.shape, 0) == offset
        pages[p, r] = jnp.where(here, row, old).astype(BF16)
        put(p, r, slot).start()

    each(lambda p, r, slot, _: fetch(p, r, slot).start())
    each(change)
    each(lambda p, r, slot, _: put(p, r, slot).wait())


def local(
    hidden,
    positions,
    cache_len,
    page_table,
    move_dest,
    paged_keys,
    paged_values,
    qkv_projection,
    query_norm_gain,
    key_gain,
    output_proj,
    input_gain,
    attn_gain,
    ffw_gain,
    final_gain,
    gate_weight,
    up_weight,
    down_weight,
):
    blocks = lax.axis_size("blk")
    kv_size = lax.axis_size("kv")
    device = lax.axis_index("blk")
    requests, model = hidden.shape
    head = query_norm_gain.shape[0]
    slots, page, _ = paged_keys.shape
    pages_per_seq = page_table.shape[1]
    capacity = max(2, (slots + blocks - 1) // blocks)
    recv_slots = blocks * capacity
    feature_rows, columns = qkv_projection.shape
    groups = columns // head - 2
    col_tiles = columns // LANES
    model_tiles = model // LANES
    assert requests == blocks

    hidden32 = hidden.astype(F32)
    scale = lax.rsqrt(jnp.mean(hidden32 * hidden32, axis=-1, keepdims=True) + EPSILON)
    start = device * feature_rows
    normed = (
        lax.dynamic_slice_in_dim(hidden, start, feature_rows, 1).astype(F32)
        * scale
        * lax.dynamic_slice_in_dim(input_gain, start, feature_rows, 0)
    ).astype(BF16)
    terms = jnp.dot(normed, qkv_projection, preferred_element_type=F32).astype(BF16)
    terms = exchange(terms.reshape(requests, col_tiles, LANES))

    cores, depth = 2, 8
    near = blocks // depth
    across = device // (depth * cores)
    along = device // cores % depth
    core = device % cores

    def index(x, z, c):
        return (x % (near // cores) * depth + z % depth) * cores + c

    def pairs(step_near, step_along):
        out = []
        for b in range(blocks):
            x, z, c = b // (depth * cores), b // cores % depth, b % cores
            out.append(
                (b, index(x + step_near // cores, z + step_along, c ^ (step_near % cores)))
            )
        return out

    to_near = [pairs(k, 0) for k in range(near)]
    to_along = [pairs(0, k) for k in range(depth)]

    vmem = pl.BlockSpec(memory_space=pltpu.VMEM)
    smem = pl.BlockSpec(memory_space=pltpu.SMEM)
    anywhere = pl.BlockSpec(memory_space=pl.ANY)

    def buffers(count):
        return [jax.ShapeDtypeStruct((recv_slots // count, page, head), BF16)] * count

    def gather(pages, order, count):
        match = order[None, :] == jnp.arange(recv_slots, dtype=jnp.int32)[:, None]
        source_of = slots + jnp.sum(jnp.where(match, slot_iota[None, :] - slots, 0), axis=1)
        return pl.pallas_call(
            gather_body,
            out_shape=buffers(count),
            in_specs=[smem, vmem],
            out_specs=[vmem] * count,
            cost_estimate=pl.CostEstimate(
                flops=0, bytes_accessed=6 * slots * page * head, transcendentals=0
            ),
        )(source_of, pages)

    def regroup(chunks, count):
        return pl.pallas_call(
            functools.partial(regroup_body, len(chunks)),
            out_shape=buffers(count),
            in_specs=[anywhere] * len(chunks),
            out_specs=[anywhere] * count,
            scratch_shapes=[pltpu.SemaphoreType.DMA((count,))],
            cost_estimate=pl.CostEstimate(
                flops=0, bytes_accessed=8 * slots * page * head, transcendentals=0
            ),
        )(*chunks)

    dest = lax.dynamic_slice_in_dim(move_dest[:, 0], device * slots, slots)
    slot_iota = jnp.arange(slots, dtype=jnp.int32)
    earlier = (dest[None, :] == dest[:, None]) & (slot_iota[None, :] < slot_iota[:, None])
    rank = jnp.sum(earlier.astype(jnp.int32), axis=1)
    step_near = (dest // (depth * cores) - across) % (near // cores) * cores + (dest % cores ^ core)
    step_along = (dest // cores - along) % depth
    keys_sends = gather(paged_keys, (step_near * depth + step_along) * capacity + rank, near)
    values_sends = gather(paged_values, (step_along * near + step_near) * capacity + rank, depth)
    terms, keys_sends, values_sends = tie(terms, keys_sends, values_sends)
    keys_first = [keys_sends[0]] + [
        lax.ppermute(keys_sends[k], "blk", to_near[k]) for k in range(1, near)
    ]
    values_first = [values_sends[0]] + [
        lax.ppermute(values_sends[k], "blk", to_along[k]) for k in range(1, depth)
    ]

    frequency = jnp.exp(-(2.0 * jnp.arange(head // 2, dtype=F32) / head) * ROPE_LOG)
    position = lax.dynamic_slice_in_dim(positions, device, 1).astype(F32)
    angles = position[:, None] * frequency[None, :]
    tile = (head // LANES, LANES)
    every, own = call(
        head_body,
        (
            jax.ShapeDtypeStruct((requests, col_tiles, LANES), BF16),
            jax.ShapeDtypeStruct((col_tiles, LANES), BF16),
        ),
        5,
        requests * columns,
        4 * requests * columns,
    )(
        terms,
        jnp.cos(angles),
        jnp.sin(angles),
        query_norm_gain.reshape(tile),
        key_gain.reshape(tile),
    )
    every = exchange(every)
    every, keys_first[1:4], values_first[1:3] = tie(every, keys_first[1:4], values_first[1:3])

    slot_ids = device * slots + jnp.arange(slots, dtype=jnp.int32)
    page_starts = jnp.arange(pages_per_seq, dtype=jnp.int32) * page
    held = jnp.clip(cache_len[:, None] - page_starts[None, :], 0, page)
    limit = jnp.sum(
        jnp.where(page_table[:, None, :] == slot_ids[None, :, None], held[:, None, :], 0), axis=-1
    ).astype(BF16)
    parts = call(
        functools.partial(attend_body, groups),
        jax.ShapeDtypeStruct((requests, columns), BF16),
        4,
        4 * groups * requests * slots * page * head,
        4 * slots * page * head,
    )(every.reshape(requests, columns), paged_keys, paged_values, limit)
    parts = exchange(parts.reshape(requests, col_tiles, LANES))
    parts, keys_first[4:6], values_first[3:6] = tie(parts, keys_first[4:6], values_first[3:6])
    attn_terms = call(
        functools.partial(merge_body, groups),
        jax.ShapeDtypeStruct((kv_size, model_tiles, LANES), F32),
        3,
        16 * groups * head * model,
        2 * groups * head * model,
    )(parts, own, output_proj)

    attn_terms = lax.all_to_all(attn_terms, "kv", split_axis=0, concat_axis=0, tiled=True)
    attn_terms, keys_first[6:], values_first[6:] = tie(
        attn_terms, keys_first[6:], values_first[6:]
    )
    keys_sends = regroup(keys_first, depth)
    values_sends = regroup(values_first, near)
    wide = (model_tiles, LANES)
    residual, ffw_in = call(
        residual_body,
        (
            jax.ShapeDtypeStruct(wide, F32),
            jax.ShapeDtypeStruct((requests,) + wide, BF16),
        ),
        4,
        model * 16,
        2 * requests * model,
    )(
        attn_terms,
        lax.dynamic_slice_in_dim(hidden, device, 1, 0).reshape(wide),
        attn_gain.reshape(wide),
        ffw_gain.reshape(wide),
    )
    ffw_in = exchange(ffw_in).reshape(requests, model)
    ffw_in, keys_sends, values_sends = tie(ffw_in, keys_sends, values_sends)
    keys_second = [keys_sends[0]] + [
        lax.ppermute(keys_sends[k], "blk", to_along[k]) for k in range(1, depth)
    ]
    values_second = [values_sends[0]] + [
        lax.ppermute(values_sends[k], "blk", to_near[k]) for k in range(1, near)
    ]
    units = gate_weight.shape[1]
    ffw_terms = call(
        ffw_body,
        jax.ShapeDtypeStruct((requests, model), BF16),
        4,
        6 * requests * units * model,
        6 * units * model,
    )(ffw_in, gate_weight, up_weight, down_weight)
    ffw_terms = exchange(ffw_terms.reshape((requests,) + wide))
    ffw_terms, keys_second[1:4], values_second[1:3] = tie(
        ffw_terms, keys_second[1:4], values_second[1:3]
    )
    out_rows = call(
        output_body,
        jax.ShapeDtypeStruct((requests,) + wide, BF16),
        3,
        requests * model,
        4 * requests * model,
    )(ffw_terms, residual, final_gain.reshape(wide))
    out_hidden = exchange(out_rows).reshape(requests, model).astype(F32)

    target = jnp.sum(
        jnp.where(
            jnp.arange(pages_per_seq, dtype=jnp.int32)[None, :] == cache_len[:, None] // page,
            page_table,
            0,
        ),
        axis=1,
    )
    all_dest = move_dest[:, 0]
    all_slots = jnp.arange(all_dest.shape[0], dtype=jnp.int32)
    target_dest = jnp.sum(
        jnp.where(all_slots[None, :] == target[:, None], all_dest[None, :], 0), axis=1
    )
    target_rank = jnp.sum(
        (
            (all_slots[None, :] // slots == target[:, None] // slots)
            & (all_slots[None, :] < target[:, None])
            & (all_dest[None, :] == target_dest[:, None])
        ).astype(jnp.int32),
        axis=1,
    )
    arrival = target // slots * capacity + target_rank
    arrive = jnp.where(target_dest == device, arrival * page + cache_len % page, -1)
    back_along = jnp.arange(depth, dtype=jnp.int32)
    back_near = jnp.arange(near, dtype=jnp.int32)

    def source_index(along_step, near_step):
        return index(
            across - near_step // cores, along - along_step, core ^ (near_step % cores)
        ).reshape(-1)

    place = jnp.stack(
        [
            source_index(back_along[:, None], back_near[None, :]),
            source_index(back_along[None, :], back_near[:, None]),
        ]
    )
    moved = jax.ShapeDtypeStruct((recv_slots, page, head), BF16)
    relocated_keys, relocated_values = pl.pallas_call(
        functools.partial(assemble_body, (depth, near), capacity),
        out_shape=[moved] * 2,
        in_specs=[smem, smem, vmem] + [anywhere] * (depth + near),
        out_specs=[anywhere] * 2,
        scratch_shapes=[
            pltpu.VMEM((2, requests, page, head), BF16),
            pltpu.SemaphoreType.DMA((2,)),
            pltpu.SemaphoreType.DMA((2, requests)),
        ],
        cost_estimate=pl.CostEstimate(
            flops=0, bytes_accessed=16 * slots * page * head, transcendentals=0
        ),
    )(place, arrive, every, *keys_second, *values_second)
    return (out_hidden, relocated_keys, relocated_values)


def solution(mesh):
    return jax.shard_map(
        local,
        mesh=mesh,
        in_specs=(
            P(),
            P(),
            P(),
            P(),
            P(),
            P("blk", None, "kv"),
            P("blk", None, "kv"),
            P("blk", "kv"),
            P(),
            P(),
            P("kv", None),
            P(),
            P(),
            P(),
            P(),
            P(None, "blk"),
            P(None, "blk"),
            P("blk", None),
        ),
        out_specs=(P(), P("blk", None, "kv"), P("blk", None, "kv")),
        check_vma=False,
    )
```

```python
import functools
import math

import jax
import jax.numpy as jnp
from jax import lax
from jax.experimental import pallas as pl
from jax.experimental.pallas import tpu as pltpu
from jax.sharding import PartitionSpec as P

EPSILON = 1e-06
QK_SCALE = 0.0625
ROPE_LOG = math.log(1000000.0)
NEG_LARGE = -1e30
LANES = 128
BF16 = jnp.bfloat16
F32 = jnp.float32


def call(body, out_shape, n_in, flops, bytes_accessed):
    vmem = pl.BlockSpec(memory_space=pltpu.VMEM)
    return pl.pallas_call(
        body,
        out_shape=out_shape,
        in_specs=[vmem] * n_in,
        out_specs=jax.tree.map(lambda _: vmem, out_shape),
        cost_estimate=pl.CostEstimate(
            flops=flops, bytes_accessed=bytes_accessed, transcendentals=0
        ),
    )


def tie(*values):
    return lax.optimization_barrier(values)


def exchange(x):
    return lax.all_to_all(x, "blk", split_axis=0, concat_axis=0, tiled=True)


def inv_rms(square_sum, width):
    return lax.rsqrt(square_sum / width + EPSILON)


def tile_sum(x):
    return jnp.sum(jnp.sum(x, axis=1, keepdims=True), axis=0, keepdims=True)


def head_body(terms_ref, cos_ref, sin_ref, qgain_ref, kgain_ref, all_ref, own_ref):
    total = jnp.sum(terms_ref[...].astype(F32), axis=0)
    total = total.astype(BF16).astype(F32)
    cosine, sine = cos_ref[...], sin_ref[...]
    rows = []
    heads = total.shape[0] // 2 - 1
    for h in range(heads):
        gain = qgain_ref[...] if h < heads - 1 else kgain_ref[...]
        pair = total[2 * h : 2 * h + 2]
        pair = pair * inv_rms(tile_sum(pair * pair), 2 * LANES) * gain
        front, back = pair[0:1], pair[1:2]
        rows.append(front * cosine - back * sine)
        rows.append(back * cosine + front * sine)
    rows.append(total[2 * heads :])
    done = jnp.concatenate(rows, axis=0).astype(BF16)
    own_ref[...] = done
    all_ref[...] = jnp.broadcast_to(done[None], all_ref.shape)


def split3(x):
    first = x.astype(BF16).astype(F32)
    second = (x - first).astype(BF16).astype(F32)
    return first, second, x - first - second


def attend_body(groups, query_ref, keys_ref, values_ref, limit_ref, out_ref):
    slots, page, width = keys_ref.shape
    requests = query_ref.shape[0]
    tokens = slots * page
    keys = keys_ref[...].reshape(tokens, width)
    values = values_ref[...].reshape(tokens, width)
    spread = (
        lax.broadcasted_iota(jnp.int32, (slots, tokens), 1) // page
        == lax.broadcasted_iota(jnp.int32, (slots, tokens), 0)
    ).astype(F32).astype(BF16)
    limit = jnp.dot(limit_ref[...], spread, preferred_element_type=F32)
    offset = (lax.broadcasted_iota(jnp.int32, (requests, tokens), 1) % page).astype(F32)
    valid = offset < limit
    lane = lax.broadcasted_iota(jnp.int32, (requests, LANES), 1)
    extra = jnp.zeros((requests, LANES), F32)
    for g in range(groups):
        scores = lax.dot_general(
            query_ref[:, g * width : (g + 1) * width],
            keys,
            (((1,), (1,)), ((), ())),
            preferred_element_type=F32,
        )
        scores = jnp.where(valid, scores * QK_SCALE, NEG_LARGE)
        peak = jnp.max(scores, axis=1, keepdims=True)
        weights = jnp.where(valid, jnp.exp(scores - peak), 0.0)
        total = jnp.sum(weights, axis=1, keepdims=True)
        mixed = jnp.dot(weights.astype(BF16), values, preferred_element_type=F32)
        out_ref[:, g * width : (g + 1) * width] = mixed.astype(BF16)
        for i, part in enumerate(split3(peak) + split3(total)):
            extra = jnp.where(lane == 8 * g + i, part, extra)
    start = groups * width
    out_ref[:, start : start + LANES] = extra.astype(BF16)
    rest = out_ref.shape[1] - start - LANES
    out_ref[:, start + LANES :] = jnp.zeros((requests, rest), BF16)


def merge_body(groups, parts_ref, own_ref, proj_ref, out_ref):
    own = own_ref[...].astype(F32)
    rows = []
    stats = parts_ref[:, 2 * groups : 2 * groups + 1, :].astype(F32)
    key = own[2 * groups : 2 * groups + 2]
    value = own[2 * groups + 2 : 2 * groups + 4]
    for g in range(groups):
        def stat(i):
            at = 8 * g + i
            return stats[:, :, at : at + 1]

        peaks = stat(0) + stat(1) + stat(2)
        sums = stat(3) + stat(4) + stat(5)
        fresh = tile_sum(own[2 * g : 2 * g + 2] * key)[None] * QK_SCALE
        peak = jnp.maximum(jnp.max(peaks, axis=0, keepdims=True), fresh)
        scale = jnp.exp(peaks - peak)
        fresh = jnp.exp(fresh - peak)
        total = jnp.sum(scale * sums, axis=0) + fresh[0]
        mixed = jnp.sum(scale * parts_ref[:, 2 * g : 2 * g + 2, :].astype(F32), axis=0)
        mixed = mixed + fresh[0].astype(BF16).astype(F32) * value
        rows.append(mixed / total)
    heads = jnp.concatenate(rows, axis=0)
    flat = jnp.concatenate([heads[i : i + 1] for i in range(heads.shape[0])], axis=1)
    flat = jnp.broadcast_to(flat, (8, flat.shape[1])).astype(BF16)
    terms = jnp.dot(flat, proj_ref[...], preferred_element_type=F32)
    tile = jnp.concatenate(
        [terms[0:1, i * LANES : (i + 1) * LANES] for i in range(out_ref.shape[1])], axis=0
    )
    out_ref[...] = jnp.broadcast_to(tile[None], out_ref.shape)


def residual_body(
    parts_ref, hidden_ref, attn_gain_ref, ffw_gain_ref, residual_ref, all_ref
):
    attn = jnp.sum(parts_ref[...], axis=0)
    width = attn.shape[0] * attn.shape[1]
    residual = (
        hidden_ref[...].astype(F32)
        + attn * inv_rms(tile_sum(attn * attn), width) * attn_gain_ref[...]
    )
    residual_ref[...] = residual
    ffw_in = residual * inv_rms(tile_sum(residual * residual), width) * ffw_gain_ref[...]
    all_ref[...] = jnp.broadcast_to(ffw_in.astype(BF16)[None], all_ref.shape)


def ffw_body(x_ref, gate_ref, up_ref, down_ref, out_ref):
    x = x_ref[...]
    gate = jnp.dot(x, gate_ref[...], preferred_element_type=F32)
    up = jnp.dot(x, up_ref[...], preferred_element_type=F32)
    units = (jax.nn.gelu(gate, approximate=True) * up).astype(BF16)
    out_ref[...] = jnp.dot(units, down_ref[...], preferred_element_type=F32).astype(BF16)


def output_body(terms_ref, residual_ref, gain_ref, all_ref):
    total = jnp.sum(terms_ref[...].astype(F32), axis=0)
    width = total.shape[0] * total.shape[1]
    row = residual_ref[...] + total * inv_rms(tile_sum(total * total), width) * gain_ref[...]
    all_ref[...] = jnp.broadcast_to(row.astype(BF16)[None], all_ref.shape)


def gather_body(source_ref, pages_ref, *outs):
    per = outs[0].shape[0]
    slots = pages_ref.shape[0]
    for j, out in enumerate(outs):

        @pl.loop(0, per, unroll=4)
        def _(q, j=j, out=out):
            source = source_ref[j * per + q]
            page = pages_ref[jnp.minimum(source, slots - 1)]
            out[q] = jnp.where(source < slots, page, jnp.zeros_like(page))


def regroup_body(count, *refs):
    ins, outs = refs[:count], refs[count:-3]
    held, in_sem, out_sem = refs[-3:]
    cap = outs[0].shape[0] // count
    for j in range(len(outs)):
        for i, chunk in enumerate(ins):
            pltpu.make_async_copy(
                chunk.at[j * cap : (j + 1) * cap], held.at[j, i * cap : (i + 1) * cap], in_sem.at[j]
            ).start()
    for j, out in enumerate(outs):
        pltpu.make_async_copy(out, held.at[j], in_sem.at[j]).wait()
        pltpu.make_async_copy(held.at[j], out, out_sem.at[j]).start()
    for j, out in enumerate(outs):
        pltpu.make_async_copy(held.at[j], out, out_sem.at[j]).wait()


def assemble_body(counts, cap, place_ref, arrive_ref, fresh_ref, *refs):
    arrays = len(counts)
    chunks, outs = refs[: sum(counts)], refs[sum(counts) : -3]
    held, in_sem, out_sem = refs[-3:]
    page = outs[0].shape[1]
    requests, tiles = fresh_ref.shape[:2]
    first = 0
    for p in range(arrays):
        inner = chunks[first].shape[0] // cap
        for j in range(counts[p]):
            for i in range(inner):
                at = place_ref[p, j * inner + i] * cap
                pltpu.make_async_copy(
                    chunks[first + j].at[i * cap : (i + 1) * cap],
                    held.at[p, pl.ds(at, cap)],
                    in_sem.at[p],
                ).start()
        first += counts[p]
    for p, out in enumerate(outs):
        pltpu.make_async_copy(out, held.at[p], in_sem.at[p]).wait()

        @pl.loop(0, requests)
        def _(r, p=p):
            where = arrive_ref[r]

            @pl.when(where >= 0)
            def _():
                at = tiles - 2 * arrays + 2 * p
                new = fresh_ref[r].astype(F32)
                row = jnp.concatenate([new[at : at + 1], new[at + 1 : at + 2]], axis=1)
                old = held[p, where // page].astype(F32)
                here = lax.broadcasted_iota(jnp.int32, old.shape, 0) == where % page
                held[p, where // page] = jnp.where(here, row, old).astype(BF16)

        pltpu.make_async_copy(held.at[p], out, out_sem.at[p]).start()
    for p, out in enumerate(outs):
        pltpu.make_async_copy(held.at[p], out, out_sem.at[p]).wait()


def local(
    hidden,
    positions,
    cache_len,
    page_table,
    move_dest,
    paged_keys,
    paged_values,
    qkv_projection,
    query_norm_gain,
    key_gain,
    output_proj,
    input_gain,
    attn_gain,
    ffw_gain,
    final_gain,
    gate_weight,
    up_weight,
    down_weight,
):
    blocks = lax.axis_size("blk")
    kv_size = lax.axis_size("kv")
    device = lax.axis_index("blk")
    requests, model = hidden.shape
    head = query_norm_gain.shape[0]
    slots, page, _ = paged_keys.shape
    pages_per_seq = page_table.shape[1]
    capacity = max(2, (slots + blocks - 1) // blocks)
    recv_slots = blocks * capacity
    feature_rows, columns = qkv_projection.shape
    groups = columns // head - 2
    col_tiles = columns // LANES
    model_tiles = model // LANES
    assert requests == blocks

    hidden32 = hidden.astype(F32)
    scale = lax.rsqrt(jnp.mean(hidden32 * hidden32, axis=-1, keepdims=True) + EPSILON)
    start = device * feature_rows
    normed = (
        lax.dynamic_slice_in_dim(hidden, start, feature_rows, 1).astype(F32)
        * scale
        * lax.dynamic_slice_in_dim(input_gain, start, feature_rows, 0)
    ).astype(BF16)
    terms = jnp.dot(normed, qkv_projection, preferred_element_type=F32).astype(BF16)
    terms = exchange(terms.reshape(requests, col_tiles, LANES))

    cores, depth = 2, 8
    near = blocks // depth
    across = device // (depth * cores)
    along = device // cores % depth
    core = device % cores

    def index(x, z, c):
        return (x % (near // cores) * depth + z % depth) * cores + c

    def pairs(step_near, step_along):
        out = []
        for b in range(blocks):
            x, z, c = b // (depth * cores), b // cores % depth, b % cores
            out.append(
                (b, index(x + step_near // cores, z + step_along, c ^ (step_near % cores)))
            )
        return out

    to_near = [pairs(k, 0) for k in range(near)]
    to_along = [pairs(0, k) for k in range(depth)]

    vmem = pl.BlockSpec(memory_space=pltpu.VMEM)
    smem = pl.BlockSpec(memory_space=pltpu.SMEM)
    anywhere = pl.BlockSpec(memory_space=pl.ANY)

    def buffers(count):
        return [jax.ShapeDtypeStruct((recv_slots // count, page, head), BF16)] * count

    def gather(pages, order, count):
        match = order[None, :] == jnp.arange(recv_slots, dtype=jnp.int32)[:, None]
        source_of = slots + jnp.sum(jnp.where(match, slot_iota[None, :] - slots, 0), axis=1)
        return pl.pallas_call(
            gather_body,
            out_shape=buffers(count),
            in_specs=[smem, vmem],
            out_specs=[vmem] * count,
            cost_estimate=pl.CostEstimate(
                flops=0, bytes_accessed=6 * slots * page * head, transcendentals=0
            ),
        )(source_of, pages)

    def regroup(chunks, count):
        return pl.pallas_call(
            functools.partial(regroup_body, len(chunks)),
            out_shape=buffers(count),
            in_specs=[anywhere] * len(chunks),
            out_specs=[anywhere] * count,
            scratch_shapes=[
                pltpu.VMEM((count, recv_slots // count, page, head), BF16),
                pltpu.SemaphoreType.DMA((count,)),
                pltpu.SemaphoreType.DMA((count,)),
            ],
            cost_estimate=pl.CostEstimate(
                flops=0, bytes_accessed=8 * slots * page * head, transcendentals=0
            ),
        )(*chunks)

    dest = lax.dynamic_slice_in_dim(move_dest[:, 0], device * slots, slots)
    slot_iota = jnp.arange(slots, dtype=jnp.int32)
    earlier = (dest[None, :] == dest[:, None]) & (slot_iota[None, :] < slot_iota[:, None])
    rank = jnp.sum(earlier.astype(jnp.int32), axis=1)
    step_near = (dest // (depth * cores) - across) % (near // cores) * cores + (dest % cores ^ core)
    step_along = (dest // cores - along) % depth
    keys_sends = gather(paged_keys, (step_near * depth + step_along) * capacity + rank, near)
    values_sends = gather(paged_values, (step_along * near + step_near) * capacity + rank, depth)
    terms, keys_sends, values_sends = tie(terms, keys_sends, values_sends)

    def permutes(sends, targets):
        return [sends[0]] + [
            lax.ppermute(sends[k], "blk", targets[k]) for k in range(1, len(sends))
        ]

    def due(value, *wanted):
        done = tie(value, *[moves[k] for moves, steps in wanted for k in steps])
        rest = iter(done[1:])
        for moves, steps in wanted:
            for k in steps:
                moves[k] = next(rest)
        return done[0]

    keys_first = permutes(keys_sends, to_near)
    values_first = permutes(values_sends, to_along)

    frequency = jnp.exp(-(2.0 * jnp.arange(head // 2, dtype=F32) / head) * ROPE_LOG)
    position = lax.dynamic_slice_in_dim(positions, device, 1).astype(F32)
    angles = position[:, None] * frequency[None, :]
    tile = (head // LANES, LANES)
    every, own = call(
        head_body,
        (
            jax.ShapeDtypeStruct((requests, col_tiles, LANES), BF16),
            jax.ShapeDtypeStruct((col_tiles, LANES), BF16),
        ),
        5,
        requests * columns,
        4 * requests * columns,
    )(
        terms,
        jnp.cos(angles),
        jnp.sin(angles),
        query_norm_gain.reshape(tile),
        key_gain.reshape(tile),
    )
    every = exchange(every)
    every = due(every, (values_first, (4, 1)), (keys_first, (4, 2, 6)))

    slot_ids = device * slots + jnp.arange(slots, dtype=jnp.int32)
    page_starts = jnp.arange(pages_per_seq, dtype=jnp.int32) * page
    held = jnp.clip(cache_len[:, None] - page_starts[None, :], 0, page)
    limit = jnp.sum(
        jnp.where(page_table[:, None, :] == slot_ids[None, :, None], held[:, None, :], 0), axis=-1
    ).astype(BF16)
    parts = call(
        functools.partial(attend_body, groups),
        jax.ShapeDtypeStruct((requests, columns), BF16),
        4,
        4 * groups * requests * slots * page * head,
        4 * slots * page * head,
    )(every.reshape(requests, columns), paged_keys, paged_values, limit)
    parts = exchange(parts.reshape(requests, col_tiles, LANES))
    parts = due(parts, (values_first, (3, 5)), (keys_first, (5, 3, 7, 1)))
    keys_sends = regroup(keys_first, depth)
    attn_terms = call(
        functools.partial(merge_body, groups),
        jax.ShapeDtypeStruct((kv_size, model_tiles, LANES), F32),
        3,
        16 * groups * head * model,
        2 * groups * head * model,
    )(parts, own, output_proj)

    attn_terms = lax.all_to_all(attn_terms, "kv", split_axis=0, concat_axis=0, tiled=True)
    attn_terms = due(attn_terms, (values_first, (2, 6, 7)))
    attn_terms, keys_sends = tie(attn_terms, keys_sends)
    keys_second = permutes(keys_sends, to_along)
    values_sends = regroup(values_first, near)
    wide = (model_tiles, LANES)
    residual, ffw_in = call(
        residual_body,
        (
            jax.ShapeDtypeStruct(wide, F32),
            jax.ShapeDtypeStruct((requests,) + wide, BF16),
        ),
        4,
        model * 16,
        2 * requests * model,
    )(
        attn_terms,
        lax.dynamic_slice_in_dim(hidden, device, 1, 0).reshape(wide),
        attn_gain.reshape(wide),
        ffw_gain.reshape(wide),
    )
    ffw_in = exchange(ffw_in).reshape(requests, model)
    ffw_in = due(ffw_in, (keys_second, (3, 5)))
    ffw_in, values_sends = tie(ffw_in, values_sends)
    values_second = permutes(values_sends, to_near)
    units = gate_weight.shape[1]
    ffw_terms = call(
        ffw_body,
        jax.ShapeDtypeStruct((requests, model), BF16),
        4,
        6 * requests * units * model,
        6 * units * model,
    )(ffw_in, gate_weight, up_weight, down_weight)
    ffw_terms = exchange(ffw_terms.reshape((requests,) + wide))
    ffw_terms = due(ffw_terms, (keys_second, (2, 6, 4)), (values_second, (4, 2)))
    out_rows = call(
        output_body,
        jax.ShapeDtypeStruct((requests,) + wide, BF16),
        3,
        requests * model,
        4 * requests * model,
    )(ffw_terms, residual, final_gain.reshape(wide))
    out_hidden = exchange(out_rows).reshape(requests, model).astype(F32)

    target = jnp.sum(
        jnp.where(
            jnp.arange(pages_per_seq, dtype=jnp.int32)[None, :] == cache_len[:, None] // page,
            page_table,
            0,
        ),
        axis=1,
    )
    all_dest = move_dest[:, 0]
    all_slots = jnp.arange(all_dest.shape[0], dtype=jnp.int32)
    target_dest = jnp.sum(
        jnp.where(all_slots[None, :] == target[:, None], all_dest[None, :], 0), axis=1
    )
    target_rank = jnp.sum(
        (
            (all_slots[None, :] // slots == target[:, None] // slots)
            & (all_slots[None, :] < target[:, None])
            & (all_dest[None, :] == target_dest[:, None])
        ).astype(jnp.int32),
        axis=1,
    )
    arrival = target // slots * capacity + target_rank
    arrive = jnp.where(target_dest == device, arrival * page + cache_len % page, -1)
    back_along = jnp.arange(depth, dtype=jnp.int32)
    back_near = jnp.arange(near, dtype=jnp.int32)

    def source_index(along_step, near_step):
        return index(
            across - near_step // cores, along - along_step, core ^ (near_step % cores)
        ).reshape(-1)

    place = jnp.stack(
        [
            source_index(back_along[:, None], back_near[None, :]),
            source_index(back_along[None, :], back_near[:, None]),
        ]
    )
    moved = jax.ShapeDtypeStruct((recv_slots, page, head), BF16)
    relocated_keys, relocated_values = pl.pallas_call(
        functools.partial(assemble_body, (depth, near), capacity),
        out_shape=[moved] * 2,
        in_specs=[smem, smem, vmem] + [anywhere] * (depth + near),
        out_specs=[anywhere] * 2,
        scratch_shapes=[
            pltpu.VMEM((2, recv_slots, page, head), BF16),
            pltpu.SemaphoreType.DMA((2,)),
            pltpu.SemaphoreType.DMA((2,)),
        ],
        cost_estimate=pl.CostEstimate(
            flops=0, bytes_accessed=16 * slots * page * head, transcendentals=0
        ),
    )(place, arrive, every, *keys_second, *values_second)
    return (out_hidden, relocated_keys, relocated_values)


def solution(mesh):
    return jax.shard_map(
        local,
        mesh=mesh,
        in_specs=(
            P(),
            P(),
            P(),
            P(),
            P(),
            P("blk", None, "kv"),
            P("blk", None, "kv"),
            P("blk", "kv"),
            P(),
            P(),
            P("kv", None),
            P(),
            P(),
            P(),
            P(),
            P(None, "blk"),
            P(None, "blk"),
            P("blk", None),
        ),
        out_specs=(P(), P("blk", None, "kv"), P("blk", None, "kv")),
        check_vma=False,
    )
```

```python
import functools
import math

import jax
import jax.numpy as jnp
from jax import lax
from jax.experimental import pallas as pl
from jax.experimental.pallas import tpu as pltpu
from jax.sharding import PartitionSpec as P

EPSILON = 1e-06
QK_SCALE = 0.0625
ROPE_LOG = math.log(1000000.0)
NEG_LARGE = -1e30
LANES = 128
BF16 = jnp.bfloat16
F32 = jnp.float32
PARAMS = pltpu.CompilerParams(vmem_limit_bytes=16 << 20)


def call(body, out_shape, n_in, flops, bytes_accessed):
    vmem = pl.BlockSpec(memory_space=pltpu.VMEM)
    return pl.pallas_call(
        body,
        out_shape=out_shape,
        in_specs=[vmem] * n_in,
        out_specs=jax.tree.map(lambda _: vmem, out_shape),
        cost_estimate=pl.CostEstimate(
            flops=flops, bytes_accessed=bytes_accessed, transcendentals=0
        ),
        compiler_params=PARAMS,
    )


def tie(*values):
    return lax.optimization_barrier(values)


def exchange(x):
    return lax.all_to_all(x, "blk", split_axis=0, concat_axis=0, tiled=True)


def inv_rms(square_sum, width):
    return lax.rsqrt(square_sum / width + EPSILON)


def tile_sum(x):
    return jnp.sum(jnp.sum(x, axis=1, keepdims=True), axis=0, keepdims=True)


def head_body(terms_ref, cos_ref, sin_ref, qgain_ref, kgain_ref, all_ref, own_ref):
    total = jnp.sum(terms_ref[...].astype(F32), axis=0)
    total = total.astype(BF16).astype(F32)
    cosine, sine = cos_ref[...], sin_ref[...]
    rows = []
    heads = total.shape[0] // 2 - 1
    for h in range(heads):
        gain = qgain_ref[...] if h < heads - 1 else kgain_ref[...]
        pair = total[2 * h : 2 * h + 2]
        pair = pair * inv_rms(tile_sum(pair * pair), 2 * LANES) * gain
        front, back = pair[0:1], pair[1:2]
        rows.append(front * cosine - back * sine)
        rows.append(back * cosine + front * sine)
    rows.append(total[2 * heads :])
    done = jnp.concatenate(rows, axis=0).astype(BF16)
    own_ref[...] = done
    all_ref[...] = jnp.broadcast_to(done[None], all_ref.shape)


def split3(x):
    first = x.astype(BF16).astype(F32)
    second = (x - first).astype(BF16).astype(F32)
    return first, second, x - first - second


def attend_body(groups, query_ref, keys_ref, values_ref, limit_ref, out_ref):
    slots, page, width = keys_ref.shape
    requests = query_ref.shape[0]
    tokens = slots * page
    keys = keys_ref[...].reshape(tokens, width)
    values = values_ref[...].reshape(tokens, width)
    spread = (
        lax.broadcasted_iota(jnp.int32, (slots, tokens), 1) // page
        == lax.broadcasted_iota(jnp.int32, (slots, tokens), 0)
    ).astype(F32).astype(BF16)
    limit = jnp.dot(limit_ref[...], spread, preferred_element_type=F32)
    offset = (lax.broadcasted_iota(jnp.int32, (requests, tokens), 1) % page).astype(F32)
    valid = offset < limit
    lane = lax.broadcasted_iota(jnp.int32, (requests, LANES), 1)
    extra = jnp.zeros((requests, LANES), F32)
    for g in range(groups):
        scores = lax.dot_general(
            query_ref[:, g * width : (g + 1) * width],
            keys,
            (((1,), (1,)), ((), ())),
            preferred_element_type=F32,
        )
        scores = jnp.where(valid, scores * QK_SCALE, NEG_LARGE)
        peak = jnp.max(scores, axis=1, keepdims=True)
        weights = jnp.where(valid, jnp.exp(scores - peak), 0.0)
        total = jnp.sum(weights, axis=1, keepdims=True)
        mixed = jnp.dot(weights.astype(BF16), values, preferred_element_type=F32)
        out_ref[:, g * width : (g + 1) * width] = mixed.astype(BF16)
        for i, part in enumerate(split3(peak) + split3(total)):
            extra = jnp.where(lane == 8 * g + i, part, extra)
    start = groups * width
    out_ref[:, start : start + LANES] = extra.astype(BF16)
    rest = out_ref.shape[1] - start - LANES
    out_ref[:, start + LANES :] = jnp.zeros((requests, rest), BF16)


def merge_body(groups, parts_ref, own_ref, proj_ref, out_ref):
    own = own_ref[...].astype(F32)
    rows = []
    stats = parts_ref[:, 2 * groups : 2 * groups + 1, :].astype(F32)
    key = own[2 * groups : 2 * groups + 2]
    value = own[2 * groups + 2 : 2 * groups + 4]
    for g in range(groups):
        def stat(i):
            at = 8 * g + i
            return stats[:, :, at : at + 1]

        peaks = stat(0) + stat(1) + stat(2)
        sums = stat(3) + stat(4) + stat(5)
        fresh = tile_sum(own[2 * g : 2 * g + 2] * key)[None] * QK_SCALE
        peak = jnp.maximum(jnp.max(peaks, axis=0, keepdims=True), fresh)
        scale = jnp.exp(peaks - peak)
        fresh = jnp.exp(fresh - peak)
        total = jnp.sum(scale * sums, axis=0) + fresh[0]
        mixed = jnp.sum(scale * parts_ref[:, 2 * g : 2 * g + 2, :].astype(F32), axis=0)
        mixed = mixed + fresh[0].astype(BF16).astype(F32) * value
        rows.append(mixed / total)
    heads = jnp.concatenate(rows, axis=0)
    flat = jnp.concatenate([heads[i : i + 1] for i in range(heads.shape[0])], axis=1)
    flat = jnp.broadcast_to(flat, (8, flat.shape[1])).astype(BF16)
    terms = jnp.dot(flat, proj_ref[...], preferred_element_type=F32)
    tile = jnp.concatenate(
        [terms[0:1, i * LANES : (i + 1) * LANES] for i in range(out_ref.shape[1])], axis=0
    )
    out_ref[...] = jnp.broadcast_to(tile[None], out_ref.shape)


def residual_body(
    parts_ref, hidden_ref, attn_gain_ref, ffw_gain_ref, residual_ref, all_ref
):
    attn = jnp.sum(parts_ref[...], axis=0)
    width = attn.shape[0] * attn.shape[1]
    residual = (
        hidden_ref[...].astype(F32)
        + attn * inv_rms(tile_sum(attn * attn), width) * attn_gain_ref[...]
    )
    residual_ref[...] = residual
    ffw_in = residual * inv_rms(tile_sum(residual * residual), width) * ffw_gain_ref[...]
    all_ref[...] = jnp.broadcast_to(ffw_in.astype(BF16)[None], all_ref.shape)


def ffw_body(x_ref, gate_ref, up_ref, down_ref, out_ref):
    x = x_ref[...]
    across = (((1,), (1,)), ((), ()))
    gate = lax.dot_general(x, gate_ref[...], across, preferred_element_type=F32)
    up = lax.dot_general(x, up_ref[...], across, preferred_element_type=F32)
    units = (jax.nn.gelu(gate, approximate=True) * up).astype(BF16)
    out_ref[...] = jnp.dot(units, down_ref[...], preferred_element_type=F32).astype(BF16)


def output_body(terms_ref, residual_ref, gain_ref, all_ref):
    total = jnp.sum(terms_ref[...].astype(F32), axis=0)
    width = total.shape[0] * total.shape[1]
    row = residual_ref[...] + total * inv_rms(tile_sum(total * total), width) * gain_ref[...]
    all_ref[...] = jnp.broadcast_to(row.astype(BF16)[None], all_ref.shape)


def gather_body(source_ref, pages_ref, *outs):
    per = outs[0].shape[0]
    slots = pages_ref.shape[0]
    for j, out in enumerate(outs):

        @pl.loop(0, per, unroll=4)
        def _(q, j=j, out=out):
            source = source_ref[j * per + q]
            page = pages_ref[jnp.minimum(source, slots - 1)]
            out[q] = jnp.where(source < slots, page, jnp.zeros_like(page))


def regroup_body(count, *refs):
    ins, outs = refs[:count], refs[count:-3]
    held, in_sem, out_sem = refs[-3:]
    cap = outs[0].shape[0] // count
    for j in range(len(outs)):
        for i, chunk in enumerate(ins):
            pltpu.make_async_copy(
                chunk.at[j * cap : (j + 1) * cap], held.at[j, i * cap : (i + 1) * cap], in_sem.at[j]
            ).start()
    for j, out in enumerate(outs):
        pltpu.make_async_copy(out, held.at[j], in_sem.at[j]).wait()
        pltpu.make_async_copy(held.at[j], out, out_sem.at[j]).start()
    for j, out in enumerate(outs):
        pltpu.make_async_copy(held.at[j], out, out_sem.at[j]).wait()


def assemble_body(counts, cap, place_ref, arrive_ref, fresh_ref, *refs):
    arrays = len(counts)
    chunks, outs = refs[: sum(counts)], refs[sum(counts) : -3]
    held, in_sem, out_sem = refs[-3:]
    page = outs[0].shape[1]
    requests, tiles = fresh_ref.shape[:2]
    first = 0
    for p in range(arrays):
        inner = chunks[first].shape[0] // cap
        for j in range(counts[p]):
            for i in range(inner):
                at = place_ref[p, j * inner + i] * cap
                pltpu.make_async_copy(
                    chunks[first + j].at[i * cap : (i + 1) * cap],
                    held.at[p, pl.ds(at, cap)],
                    in_sem.at[p],
                ).start()
        first += counts[p]
    for p, out in enumerate(outs):
        pltpu.make_async_copy(out, held.at[p], in_sem.at[p]).wait()

        @pl.loop(0, requests)
        def _(r, p=p):
            where = arrive_ref[r]

            @pl.when(where >= 0)
            def _():
                at = tiles - 2 * arrays + 2 * p
                new = fresh_ref[r].astype(F32)
                row = jnp.concatenate([new[at : at + 1], new[at + 1 : at + 2]], axis=1)
                old = held[p, where // page].astype(F32)
                here = lax.broadcasted_iota(jnp.int32, old.shape, 0) == where % page
                held[p, where // page] = jnp.where(here, row, old).astype(BF16)

        pltpu.make_async_copy(held.at[p], out, out_sem.at[p]).start()
    for p, out in enumerate(outs):
        pltpu.make_async_copy(held.at[p], out, out_sem.at[p]).wait()


def local(
    hidden,
    positions,
    cache_len,
    page_table,
    move_dest,
    paged_keys,
    paged_values,
    qkv_projection,
    query_norm_gain,
    key_gain,
    output_proj,
    input_gain,
    attn_gain,
    ffw_gain,
    final_gain,
    gate_weight,
    up_weight,
    down_weight,
):
    blocks = lax.axis_size("blk")
    kv_size = lax.axis_size("kv")
    device = lax.axis_index("blk")
    requests, model = hidden.shape
    head = query_norm_gain.shape[0]
    slots, page, _ = paged_keys.shape
    pages_per_seq = page_table.shape[1]
    capacity = max(2, (slots + blocks - 1) // blocks)
    recv_slots = blocks * capacity
    feature_rows, columns = qkv_projection.shape
    groups = columns // head - 2
    col_tiles = columns // LANES
    model_tiles = model // LANES
    assert requests == blocks

    hidden32 = hidden.astype(F32)
    scale = lax.rsqrt(jnp.mean(hidden32 * hidden32, axis=-1, keepdims=True) + EPSILON)
    start = device * feature_rows
    normed = (
        lax.dynamic_slice_in_dim(hidden, start, feature_rows, 1).astype(F32)
        * scale
        * lax.dynamic_slice_in_dim(input_gain, start, feature_rows, 0)
    ).astype(BF16)
    terms = jnp.dot(normed, qkv_projection, preferred_element_type=F32).astype(BF16)
    terms = exchange(terms.reshape(requests, col_tiles, LANES))

    cores, depth = 2, 8
    near = blocks // depth
    across = device // (depth * cores)
    along = device // cores % depth
    core = device % cores

    def index(x, z, c):
        return (x % (near // cores) * depth + z % depth) * cores + c

    def pairs(step_near, step_along):
        out = []
        for b in range(blocks):
            x, z, c = b // (depth * cores), b // cores % depth, b % cores
            out.append(
                (b, index(x + step_near // cores, z + step_along, c ^ (step_near % cores)))
            )
        return out

    to_near = [pairs(k, 0) for k in range(near)]
    to_along = [pairs(0, k) for k in range(depth)]

    vmem = pl.BlockSpec(memory_space=pltpu.VMEM)
    smem = pl.BlockSpec(memory_space=pltpu.SMEM)
    anywhere = pl.BlockSpec(memory_space=pl.ANY)

    def buffers(count):
        return [jax.ShapeDtypeStruct((recv_slots // count, page, head), BF16)] * count

    def gather(pages, order, count):
        match = order[None, :] == jnp.arange(recv_slots, dtype=jnp.int32)[:, None]
        source_of = slots + jnp.sum(jnp.where(match, slot_iota[None, :] - slots, 0), axis=1)
        return pl.pallas_call(
            gather_body,
            out_shape=buffers(count),
            in_specs=[smem, vmem],
            out_specs=[vmem] * count,
            cost_estimate=pl.CostEstimate(
                flops=0, bytes_accessed=6 * slots * page * head, transcendentals=0
            ),
compiler_params=PARAMS,
        )(source_of, pages)

    def regroup(chunks, count):
        return pl.pallas_call(
            functools.partial(regroup_body, len(chunks)),
            out_shape=buffers(count),
            in_specs=[anywhere] * len(chunks),
            out_specs=[anywhere] * count,
            scratch_shapes=[
                pltpu.VMEM((count, recv_slots // count, page, head), BF16),
                pltpu.SemaphoreType.DMA((count,)),
                pltpu.SemaphoreType.DMA((count,)),
            ],
            cost_estimate=pl.CostEstimate(
                flops=0, bytes_accessed=8 * slots * page * head, transcendentals=0
            ),
compiler_params=PARAMS,
        )(*chunks)

    dest = lax.dynamic_slice_in_dim(move_dest[:, 0], device * slots, slots)
    slot_iota = jnp.arange(slots, dtype=jnp.int32)
    earlier = (dest[None, :] == dest[:, None]) & (slot_iota[None, :] < slot_iota[:, None])
    rank = jnp.sum(earlier.astype(jnp.int32), axis=1)
    step_near = (dest // (depth * cores) - across) % (near // cores) * cores + (dest % cores ^ core)
    step_along = (dest // cores - along) % depth
    keys_sends = gather(paged_keys, (step_near * depth + step_along) * capacity + rank, near)
    values_sends = gather(paged_values, (step_along * near + step_near) * capacity + rank, depth)
    terms, keys_sends, values_sends = tie(terms, keys_sends, values_sends)

    def permutes(sends, targets):
        return [sends[0]] + [
            lax.ppermute(sends[k], "blk", targets[k]) for k in range(1, len(sends))
        ]

    def due(value, *wanted):
        done = tie(value, *[moves[k] for moves, steps in wanted for k in steps])
        rest = iter(done[1:])
        for moves, steps in wanted:
            for k in steps:
                moves[k] = next(rest)
        return done[0]

    frequency = jnp.exp(-(2.0 * jnp.arange(head // 2, dtype=F32) / head) * ROPE_LOG)
    position = lax.dynamic_slice_in_dim(positions, device, 1).astype(F32)
    angles = position[:, None] * frequency[None, :]
    tile = (head // LANES, LANES)
    every, own = call(
        head_body,
        (
            jax.ShapeDtypeStruct((requests, col_tiles, LANES), BF16),
            jax.ShapeDtypeStruct((col_tiles, LANES), BF16),
        ),
        5,
        requests * columns,
        4 * requests * columns,
    )(
        terms,
        jnp.cos(angles),
        jnp.sin(angles),
        query_norm_gain.reshape(tile),
        key_gain.reshape(tile),
    )
    every, *sends = tie(every, *keys_sends, *values_sends)
    keys_first = permutes(sends[:near], to_near)
    values_first = permutes(sends[near:], to_along)
    every = exchange(every)
    every = due(every, (values_first, (4, 1)), (keys_first, (4, 2, 6)))

    slot_ids = device * slots + jnp.arange(slots, dtype=jnp.int32)
    page_starts = jnp.arange(pages_per_seq, dtype=jnp.int32) * page
    held = jnp.clip(cache_len[:, None] - page_starts[None, :], 0, page)
    limit = jnp.sum(
        jnp.where(page_table[:, None, :] == slot_ids[None, :, None], held[:, None, :], 0), axis=-1
    ).astype(BF16)
    parts = call(
        functools.partial(attend_body, groups),
        jax.ShapeDtypeStruct((requests, columns), BF16),
        4,
        4 * groups * requests * slots * page * head,
        4 * slots * page * head,
    )(every.reshape(requests, columns), paged_keys, paged_values, limit)
    parts = exchange(parts.reshape(requests, col_tiles, LANES))
    parts = due(parts, (values_first, (3, 5)), (keys_first, (5, 3, 7, 1)))
    keys_sends = regroup(keys_first, depth)
    attn_terms = call(
        functools.partial(merge_body, groups),
        jax.ShapeDtypeStruct((kv_size, model_tiles, LANES), F32),
        3,
        16 * groups * head * model,
        2 * groups * head * model,
    )(parts, own, output_proj)

    attn_terms = lax.all_to_all(attn_terms, "kv", split_axis=0, concat_axis=0, tiled=True)
    attn_terms = due(attn_terms, (values_first, (2, 6, 7)))
    attn_terms, keys_sends = tie(attn_terms, keys_sends)
    keys_second = permutes(keys_sends, to_along)
    values_sends = regroup(values_first, near)
    wide = (model_tiles, LANES)
    residual, ffw_in = call(
        residual_body,
        (
            jax.ShapeDtypeStruct(wide, F32),
            jax.ShapeDtypeStruct((requests,) + wide, BF16),
        ),
        4,
        model * 16,
        2 * requests * model,
    )(
        attn_terms,
        lax.dynamic_slice_in_dim(hidden, device, 1, 0).reshape(wide),
        attn_gain.reshape(wide),
        ffw_gain.reshape(wide),
    )
    ffw_in = exchange(ffw_in).reshape(requests, model)
    ffw_in = due(ffw_in, (keys_second, (2, 6)))
    ffw_in, values_sends = tie(ffw_in, values_sends)
    values_second = permutes(values_sends, to_near)
    units = gate_weight.shape[1]
    ffw_terms = call(
        ffw_body,
        jax.ShapeDtypeStruct((requests, model), BF16),
        4,
        6 * requests * units * model,
        6 * units * model,
    )(ffw_in, gate_weight.T, up_weight.T, down_weight)
    ffw_terms = exchange(ffw_terms.reshape((requests,) + wide))
    ffw_terms = due(ffw_terms, (keys_second, (3, 5)), (values_second, (4, 2, 6)))
    out_rows = call(
        output_body,
        jax.ShapeDtypeStruct((requests,) + wide, BF16),
        3,
        requests * model,
        4 * requests * model,
    )(ffw_terms, residual, final_gain.reshape(wide))
    out_hidden = exchange(out_rows).reshape(requests, model).astype(F32)

    target = jnp.sum(
        jnp.where(
            jnp.arange(pages_per_seq, dtype=jnp.int32)[None, :] == cache_len[:, None] // page,
            page_table,
            0,
        ),
        axis=1,
    )
    all_dest = move_dest[:, 0]
    all_slots = jnp.arange(all_dest.shape[0], dtype=jnp.int32)
    target_dest = jnp.sum(
        jnp.where(all_slots[None, :] == target[:, None], all_dest[None, :], 0), axis=1
    )
    target_rank = jnp.sum(
        (
            (all_slots[None, :] // slots == target[:, None] // slots)
            & (all_slots[None, :] < target[:, None])
            & (all_dest[None, :] == target_dest[:, None])
        ).astype(jnp.int32),
        axis=1,
    )
    arrival = target // slots * capacity + target_rank
    arrive = jnp.where(target_dest == device, arrival * page + cache_len % page, -1)
    back_along = jnp.arange(depth, dtype=jnp.int32)
    back_near = jnp.arange(near, dtype=jnp.int32)

    def source_index(along_step, near_step):
        return index(
            across - near_step // cores, along - along_step, core ^ (near_step % cores)
        ).reshape(-1)

    place = jnp.stack(
        [
            source_index(back_along[:, None], back_near[None, :]),
            source_index(back_along[None, :], back_near[:, None]),
        ]
    )
    moved = jax.ShapeDtypeStruct((recv_slots, page, head), BF16)
    relocated_keys, relocated_values = pl.pallas_call(
        functools.partial(assemble_body, (depth, near), capacity),
        out_shape=[moved] * 2,
        in_specs=[smem, smem, vmem] + [anywhere] * (depth + near),
        out_specs=[anywhere] * 2,
        scratch_shapes=[
            pltpu.VMEM((2, recv_slots, page, head), BF16),
            pltpu.SemaphoreType.DMA((2,)),
            pltpu.SemaphoreType.DMA((2,)),
        ],
        cost_estimate=pl.CostEstimate(
            flops=0, bytes_accessed=16 * slots * page * head, transcendentals=0
        ),
compiler_params=PARAMS,
    )(place, arrive, every, *keys_second, *values_second)
    return (out_hidden, relocated_keys, relocated_values)


def solution(mesh):
    return jax.shard_map(
        local,
        mesh=mesh,
        in_specs=(
            P(),
            P(),
            P(),
            P(),
            P(),
            P("blk", None, "kv"),
            P("blk", None, "kv"),
            P("blk", "kv"),
            P(),
            P(),
            P("kv", None),
            P(),
            P(),
            P(),
            P(),
            P(None, "blk"),
            P(None, "blk"),
            P("blk", None),
        ),
        out_specs=(P(), P("blk", None, "kv"), P("blk", None, "kv")),
        check_vma=False,
    )
```

```python
import functools
import math

import jax
import jax.numpy as jnp
from jax import lax
from jax.experimental import pallas as pl
from jax.experimental.pallas import tpu as pltpu
from jax.sharding import PartitionSpec as P

EPSILON = 1e-06
QK_SCALE = 0.0625
ROPE_LOG = math.log(1000000.0)
NEG_LARGE = -1e30
LANES = 128
BF16 = jnp.bfloat16
F32 = jnp.float32
PARAMS = pltpu.CompilerParams(vmem_limit_bytes=16 << 20)


def call(body, out_shape, n_in, flops, bytes_accessed):
    vmem = pl.BlockSpec(memory_space=pltpu.VMEM)
    return pl.pallas_call(
        body,
        out_shape=out_shape,
        in_specs=[vmem] * n_in,
        out_specs=jax.tree.map(lambda _: vmem, out_shape),
        cost_estimate=pl.CostEstimate(
            flops=flops, bytes_accessed=bytes_accessed, transcendentals=0
        ),
        compiler_params=PARAMS,
    )


def tie(*values):
    return lax.optimization_barrier(values)


def exchange(x):
    return lax.all_to_all(x, "blk", split_axis=0, concat_axis=0, tiled=True)


def inv_rms(square_sum, width):
    return lax.rsqrt(square_sum / width + EPSILON)


def tile_sum(x):
    return jnp.sum(jnp.sum(x, axis=1, keepdims=True), axis=0, keepdims=True)


def head_body(terms_ref, cos_ref, sin_ref, qgain_ref, kgain_ref, all_ref, own_ref):
    total = jnp.sum(terms_ref[...].astype(F32), axis=0)
    total = total.astype(BF16).astype(F32)
    cosine, sine = cos_ref[...], sin_ref[...]
    rows = []
    heads = total.shape[0] // 2 - 1
    for h in range(heads):
        gain = qgain_ref[...] if h < heads - 1 else kgain_ref[...]
        pair = total[2 * h : 2 * h + 2]
        pair = pair * inv_rms(tile_sum(pair * pair), 2 * LANES) * gain
        front, back = pair[0:1], pair[1:2]
        rows.append(front * cosine - back * sine)
        rows.append(back * cosine + front * sine)
    rows.append(total[2 * heads :])
    done = jnp.concatenate(rows, axis=0).astype(BF16)
    own_ref[...] = done
    all_ref[...] = jnp.broadcast_to(done[None], all_ref.shape)


def split3(x):
    first = x.astype(BF16).astype(F32)
    second = (x - first).astype(BF16).astype(F32)
    return first, second, x - first - second


def attend_body(groups, query_ref, keys_ref, values_ref, limit_ref, out_ref):
    slots, page, width = keys_ref.shape
    requests = query_ref.shape[0]
    tokens = slots * page
    keys = keys_ref[...].reshape(tokens, width)
    values = values_ref[...].reshape(tokens, width)
    spread = (
        lax.broadcasted_iota(jnp.int32, (slots, tokens), 1) // page
        == lax.broadcasted_iota(jnp.int32, (slots, tokens), 0)
    ).astype(F32).astype(BF16)
    limit = jnp.dot(limit_ref[...], spread, preferred_element_type=F32)
    offset = (lax.broadcasted_iota(jnp.int32, (requests, tokens), 1) % page).astype(F32)
    valid = offset < limit
    lane = lax.broadcasted_iota(jnp.int32, (requests, LANES), 1)
    extra = jnp.zeros((requests, LANES), F32)
    for g in range(groups):
        scores = lax.dot_general(
            query_ref[:, g * width : (g + 1) * width],
            keys,
            (((1,), (1,)), ((), ())),
            preferred_element_type=F32,
        )
        scores = jnp.where(valid, scores * QK_SCALE, NEG_LARGE)
        peak = jnp.max(scores, axis=1, keepdims=True)
        weights = jnp.where(valid, jnp.exp(scores - peak), 0.0)
        total = jnp.sum(weights, axis=1, keepdims=True)
        mixed = jnp.dot(weights.astype(BF16), values, preferred_element_type=F32)
        out_ref[:, g * width : (g + 1) * width] = mixed.astype(BF16)
        for i, part in enumerate(split3(peak) + split3(total)):
            extra = jnp.where(lane == 8 * g + i, part, extra)
    start = groups * width
    out_ref[:, start : start + LANES] = extra.astype(BF16)
    rest = out_ref.shape[1] - start - LANES
    out_ref[:, start + LANES :] = jnp.zeros((requests, rest), BF16)


def merge_body(groups, parts_ref, own_ref, proj_ref, out_ref):
    own = own_ref[...].astype(F32)
    rows = []
    stats = parts_ref[:, 2 * groups : 2 * groups + 1, :].astype(F32)
    key = own[2 * groups : 2 * groups + 2]
    value = own[2 * groups + 2 : 2 * groups + 4]
    for g in range(groups):
        def stat(i):
            at = 8 * g + i
            return stats[:, :, at : at + 1]

        peaks = stat(0) + stat(1) + stat(2)
        sums = stat(3) + stat(4) + stat(5)
        fresh = tile_sum(own[2 * g : 2 * g + 2] * key)[None] * QK_SCALE
        peak = jnp.maximum(jnp.max(peaks, axis=0, keepdims=True), fresh)
        scale = jnp.exp(peaks - peak)
        fresh = jnp.exp(fresh - peak)
        total = jnp.sum(scale * sums, axis=0) + fresh[0]
        mixed = jnp.sum(scale * parts_ref[:, 2 * g : 2 * g + 2, :].astype(F32), axis=0)
        mixed = mixed + fresh[0].astype(BF16).astype(F32) * value
        rows.append(mixed / total)
    heads = jnp.concatenate(rows, axis=0)
    flat = jnp.concatenate([heads[i : i + 1] for i in range(heads.shape[0])], axis=1)
    flat = jnp.broadcast_to(flat, (8, flat.shape[1])).astype(BF16)
    terms = jnp.dot(flat, proj_ref[...], preferred_element_type=F32)
    out_ref[...] = jnp.concatenate(
        [terms[0:1, i * LANES : (i + 1) * LANES] for i in range(out_ref.shape[0])], axis=0
    )


def residual_body(*refs):
    hidden_ref, attn_gain_ref, ffw_gain_ref, residual_ref, all_ref = refs[-5:]
    parts = [ref[...] for ref in refs[:-5]]
    while len(parts) > 1:
        half = len(parts) // 2
        parts = [parts[i] + parts[i + half] for i in range(half)]
    attn = parts[0]
    width = attn.shape[0] * attn.shape[1]
    residual = (
        hidden_ref[...].astype(F32)
        + attn * inv_rms(tile_sum(attn * attn), width) * attn_gain_ref[...]
    )
    residual_ref[...] = residual
    ffw_in = residual * inv_rms(tile_sum(residual * residual), width) * ffw_gain_ref[...]
    all_ref[...] = jnp.broadcast_to(ffw_in.astype(BF16)[None], all_ref.shape)


def ffw_body(x_ref, gate_ref, up_ref, down_ref, out_ref):
    x = x_ref[...]
    across = (((1,), (1,)), ((), ()))
    gate = lax.dot_general(x, gate_ref[...], across, preferred_element_type=F32)
    up = lax.dot_general(x, up_ref[...], across, preferred_element_type=F32)
    units = (jax.nn.gelu(gate, approximate=True) * up).astype(BF16)
    out_ref[...] = jnp.dot(units, down_ref[...], preferred_element_type=F32).astype(BF16)


def output_body(terms_ref, residual_ref, gain_ref, all_ref):
    total = jnp.sum(terms_ref[...].astype(F32), axis=0)
    width = total.shape[0] * total.shape[1]
    row = residual_ref[...] + total * inv_rms(tile_sum(total * total), width) * gain_ref[...]
    all_ref[...] = jnp.broadcast_to(row.astype(BF16)[None], all_ref.shape)


def send_body(tile, source_ref, fresh_at_ref, fresh_ref, pages_ref, out_ref):
    slots, page, _ = pages_ref.shape

    @pl.loop(0, out_ref.shape[0], unroll=4)
    def _(q):
        source = source_ref[q]
        old = pages_ref[jnp.minimum(source, slots - 1)]
        out_ref[q] = jnp.where(source < slots, old, jnp.zeros_like(old))

    @pl.loop(0, fresh_ref.shape[0])
    def _(r):
        where = fresh_at_ref[r]

        @pl.when(where >= 0)
        def _():
            new = fresh_ref[r].astype(F32)
            row = jnp.concatenate([new[tile : tile + 1], new[tile + 1 : tile + 2]], axis=1)
            old = out_ref[where // page].astype(F32)
            here = lax.broadcasted_iota(jnp.int32, old.shape, 0) == where % page
            out_ref[where // page] = jnp.where(here, row, old).astype(BF16)


def copy_body(in_ref, out_ref):
    out_ref[...] = in_ref[...]


def local(
    hidden,
    positions,
    cache_len,
    page_table,
    move_dest,
    paged_keys,
    paged_values,
    qkv_projection,
    query_norm_gain,
    key_gain,
    output_proj,
    input_gain,
    attn_gain,
    ffw_gain,
    final_gain,
    gate_weight,
    up_weight,
    down_weight,
):
    blocks = lax.axis_size("blk")
    kv_size = lax.axis_size("kv")
    device = lax.axis_index("blk")
    requests, model = hidden.shape
    head = query_norm_gain.shape[0]
    slots, page, _ = paged_keys.shape
    pages_per_seq = page_table.shape[1]
    capacity = max(2, (slots + blocks - 1) // blocks)
    recv_slots = blocks * capacity
    feature_rows, columns = qkv_projection.shape
    groups = columns // head - 2
    col_tiles = columns // LANES
    model_tiles = model // LANES
    assert requests == blocks

    hidden32 = hidden.astype(F32)
    scale = lax.rsqrt(jnp.mean(hidden32 * hidden32, axis=-1, keepdims=True) + EPSILON)
    start = device * feature_rows
    normed = (
        lax.dynamic_slice_in_dim(hidden, start, feature_rows, 1).astype(F32)
        * scale
        * lax.dynamic_slice_in_dim(input_gain, start, feature_rows, 0)
    ).astype(BF16)
    terms = jnp.dot(normed, qkv_projection, preferred_element_type=F32).astype(BF16)
    terms = exchange(terms.reshape(requests, col_tiles, LANES))

    frequency = jnp.exp(-(2.0 * jnp.arange(head // 2, dtype=F32) / head) * ROPE_LOG)
    position = lax.dynamic_slice_in_dim(positions, device, 1).astype(F32)
    angles = position[:, None] * frequency[None, :]
    tile = (head // LANES, LANES)
    every, own = call(
        head_body,
        (
            jax.ShapeDtypeStruct((requests, col_tiles, LANES), BF16),
            jax.ShapeDtypeStruct((col_tiles, LANES), BF16),
        ),
        5,
        requests * columns,
        4 * requests * columns,
    )(
        terms,
        jnp.cos(angles),
        jnp.sin(angles),
        query_norm_gain.reshape(tile),
        key_gain.reshape(tile),
    )
    every = exchange(every)

    dest = lax.dynamic_slice_in_dim(move_dest[:, 0], device * slots, slots)
    slot_iota = jnp.arange(slots, dtype=jnp.int32)
    earlier = (dest[None, :] == dest[:, None]) & (slot_iota[None, :] < slot_iota[:, None])
    order = dest * capacity + jnp.sum(earlier.astype(jnp.int32), axis=1)
    match = order[None, :] == jnp.arange(recv_slots, dtype=jnp.int32)[:, None]
    source_of = slots + jnp.sum(jnp.where(match, slot_iota[None, :] - slots, 0), axis=1)
    target = jnp.sum(
        jnp.where(
            jnp.arange(pages_per_seq, dtype=jnp.int32)[None, :] == cache_len[:, None] // page,
            page_table,
            0,
        ),
        axis=1,
    )
    mine = (target - device * slots)[:, None] == slot_iota[None, :]
    fresh_at = jnp.sum(
        jnp.where(mine, order[None, :] * page + cache_len[:, None] % page + 1, 0), axis=1
    ) - 1
    vmem = pl.BlockSpec(memory_space=pltpu.VMEM)
    smem = pl.BlockSpec(memory_space=pltpu.SMEM)

    def sends(pages, tile):
        out = pl.pallas_call(
            functools.partial(send_body, tile),
            out_shape=jax.ShapeDtypeStruct((recv_slots, page, head), BF16),
            in_specs=[smem, smem, vmem, vmem],
            out_specs=vmem,
            cost_estimate=pl.CostEstimate(
                flops=0, bytes_accessed=6 * slots * page * head, transcendentals=0
            ),
        )(source_of, fresh_at, every, pages)
        return out.reshape(blocks, capacity, page, head)

    keys_send = sends(paged_keys, 2 * groups)
    values_send = sends(paged_values, 2 * groups + 2)

    slot_ids = device * slots + jnp.arange(slots, dtype=jnp.int32)
    page_starts = jnp.arange(pages_per_seq, dtype=jnp.int32) * page
    held = jnp.clip(cache_len[:, None] - page_starts[None, :], 0, page)
    limit = jnp.sum(
        jnp.where(page_table[:, None, :] == slot_ids[None, :, None], held[:, None, :], 0), axis=-1
    ).astype(BF16)
    parts = call(
        functools.partial(attend_body, groups),
        jax.ShapeDtypeStruct((requests, columns), BF16),
        4,
        4 * groups * requests * slots * page * head,
        4 * slots * page * head,
    )(every.reshape(requests, columns), paged_keys, paged_values, limit)
    parts = exchange(parts.reshape(requests, col_tiles, LANES))
    parts, keys_send = tie(parts, keys_send)
    relocated_keys = exchange(keys_send)
    attn_terms = call(
        functools.partial(merge_body, groups),
        jax.ShapeDtypeStruct((model_tiles, LANES), F32),
        3,
        16 * groups * head * model,
        2 * groups * head * model,
    )(parts, own, output_proj)

    everyone = [attn_terms] + [
        lax.ppermute(attn_terms, "kv", [(i, (i + d) % kv_size) for i in range(kv_size)])
        for d in range(1, kv_size)
    ]
    wide = (model_tiles, LANES)
    residual, ffw_in = call(
        residual_body,
        (
            jax.ShapeDtypeStruct(wide, F32),
            jax.ShapeDtypeStruct((requests,) + wide, BF16),
        ),
        kv_size + 3,
        model * 16,
        2 * requests * model,
    )(
        *everyone,
        lax.dynamic_slice_in_dim(hidden, device, 1, 0).reshape(wide),
        attn_gain.reshape(wide),
        ffw_gain.reshape(wide),
    )
    ffw_in, relocated_keys = tie(ffw_in, relocated_keys)
    ffw_in = exchange(ffw_in).reshape(requests, model)
    units = gate_weight.shape[1]
    ffw_terms = call(
        ffw_body,
        jax.ShapeDtypeStruct((requests, model), BF16),
        4,
        6 * requests * units * model,
        6 * units * model,
    )(ffw_in, gate_weight.T, up_weight.T, down_weight)
    ffw_terms = exchange(ffw_terms.reshape((requests,) + wide))
    out_rows = call(
        output_body,
        jax.ShapeDtypeStruct((requests,) + wide, BF16),
        3,
        requests * model,
        4 * requests * model,
    )(ffw_terms, residual, final_gain.reshape(wide))
    out_rows = exchange(out_rows)
    out_rows, values_send = tie(out_rows, values_send)
    out_hidden = out_rows.reshape(requests, model).astype(F32)
    moved = (recv_slots, page, head)
    relocated_keys = call(
        copy_body,
        jax.ShapeDtypeStruct(moved, BF16),
        1,
        0,
        8 * slots * page * head,
    )(relocated_keys.reshape(moved))
    relocated_values = exchange(values_send).reshape(moved)
    return (out_hidden, relocated_keys, relocated_values)


def solution(mesh):
    return jax.shard_map(
        local,
        mesh=mesh,
        in_specs=(
            P(),
            P(),
            P(),
            P(),
            P(),
            P("blk", None, "kv"),
            P("blk", None, "kv"),
            P("blk", "kv"),
            P(),
            P(),
            P("kv", None),
            P(),
            P(),
            P(),
            P(),
            P(None, "blk"),
            P(None, "blk"),
            P("blk", None),
        ),
        out_specs=(P(), P("blk", None, "kv"), P("blk", None, "kv")),
        check_vma=False,
    )
```

```python
import functools
import math

import jax
import jax.numpy as jnp
from jax import lax
from jax.experimental import pallas as pl
from jax.experimental.pallas import tpu as pltpu
from jax.sharding import PartitionSpec as P

EPSILON = 1e-06
QK_SCALE = 0.0625
ROPE_LOG = math.log(1000000.0)
NEG_LARGE = -1e30
LANES = 128
BF16 = jnp.bfloat16
F32 = jnp.float32
PARAMS = pltpu.CompilerParams(vmem_limit_bytes=16 << 20)


def call(body, out_shape, n_in, flops, bytes_accessed):
    vmem = pl.BlockSpec(memory_space=pltpu.VMEM)
    return pl.pallas_call(
        body,
        out_shape=out_shape,
        in_specs=[vmem] * n_in,
        out_specs=jax.tree.map(lambda _: vmem, out_shape),
        cost_estimate=pl.CostEstimate(
            flops=flops, bytes_accessed=bytes_accessed, transcendentals=0
        ),
        compiler_params=PARAMS,
    )


def tie(*values):
    return lax.optimization_barrier(values)


def exchange(x):
    return lax.all_to_all(x, "blk", split_axis=0, concat_axis=0, tiled=True)


def inv_rms(square_sum, width):
    return lax.rsqrt(square_sum / width + EPSILON)


def tile_sum(x):
    return jnp.sum(jnp.sum(x, axis=1, keepdims=True), axis=0, keepdims=True)


def head_body(terms_ref, cos_ref, sin_ref, qgain_ref, kgain_ref, all_ref, own_ref):
    total = jnp.sum(terms_ref[...].astype(F32), axis=0)
    total = total.astype(BF16).astype(F32)
    cosine, sine = cos_ref[...], sin_ref[...]
    rows = []
    heads = total.shape[0] // 2 - 1
    for h in range(heads):
        gain = qgain_ref[...] if h < heads - 1 else kgain_ref[...]
        pair = total[2 * h : 2 * h + 2]
        pair = pair * inv_rms(tile_sum(pair * pair), 2 * LANES) * gain
        front, back = pair[0:1], pair[1:2]
        rows.append(front * cosine - back * sine)
        rows.append(back * cosine + front * sine)
    rows.append(total[2 * heads :])
    done = jnp.concatenate(rows, axis=0).astype(BF16)
    own_ref[...] = done
    all_ref[...] = jnp.broadcast_to(done[None], all_ref.shape)


def split3(x):
    first = x.astype(BF16).astype(F32)
    second = (x - first).astype(BF16).astype(F32)
    return first, second, x - first - second


def attend_body(groups, query_ref, keys_ref, values_ref, limit_ref, out_ref):
    slots, page, width = keys_ref.shape
    requests = query_ref.shape[0]
    tokens = slots * page
    keys = keys_ref[...].reshape(tokens, width)
    values = values_ref[...].reshape(tokens, width)
    spread = (
        lax.broadcasted_iota(jnp.int32, (slots, tokens), 1) // page
        == lax.broadcasted_iota(jnp.int32, (slots, tokens), 0)
    ).astype(F32).astype(BF16)
    limit = jnp.dot(limit_ref[...], spread, preferred_element_type=F32)
    offset = (lax.broadcasted_iota(jnp.int32, (requests, tokens), 1) % page).astype(F32)
    valid = offset < limit
    lane = lax.broadcasted_iota(jnp.int32, (requests, LANES), 1)
    extra = jnp.zeros((requests, LANES), F32)
    for g in range(groups):
        scores = lax.dot_general(
            query_ref[:, g * width : (g + 1) * width],
            keys,
            (((1,), (1,)), ((), ())),
            preferred_element_type=F32,
        )
        scores = jnp.where(valid, scores * QK_SCALE, NEG_LARGE)
        peak = jnp.max(scores, axis=1, keepdims=True)
        weights = jnp.where(valid, jnp.exp(scores - peak), 0.0)
        total = jnp.sum(weights, axis=1, keepdims=True)
        mixed = jnp.dot(weights.astype(BF16), values, preferred_element_type=F32)
        out_ref[:, g * width : (g + 1) * width] = mixed.astype(BF16)
        for i, part in enumerate(split3(peak) + split3(total)):
            extra = jnp.where(lane == 8 * g + i, part, extra)
    start = groups * width
    out_ref[:, start : start + LANES] = extra.astype(BF16)
    rest = out_ref.shape[1] - start - LANES
    out_ref[:, start + LANES :] = jnp.zeros((requests, rest), BF16)


def merge_body(groups, parts_ref, own_ref, proj_ref, out_ref):
    own = own_ref[...].astype(F32)
    rows = []
    stats = parts_ref[:, 2 * groups : 2 * groups + 1, :].astype(F32)
    key = own[2 * groups : 2 * groups + 2]
    value = own[2 * groups + 2 : 2 * groups + 4]
    for g in range(groups):
        def stat(i):
            at = 8 * g + i
            return stats[:, :, at : at + 1]

        peaks = stat(0) + stat(1) + stat(2)
        sums = stat(3) + stat(4) + stat(5)
        fresh = tile_sum(own[2 * g : 2 * g + 2] * key)[None] * QK_SCALE
        peak = jnp.maximum(jnp.max(peaks, axis=0, keepdims=True), fresh)
        scale = jnp.exp(peaks - peak)
        fresh = jnp.exp(fresh - peak)
        total = jnp.sum(scale * sums, axis=0) + fresh[0]
        mixed = jnp.sum(scale * parts_ref[:, 2 * g : 2 * g + 2, :].astype(F32), axis=0)
        mixed = mixed + fresh[0].astype(BF16).astype(F32) * value
        rows.append(mixed / total)
    heads = jnp.concatenate(rows, axis=0)
    flat = jnp.concatenate([heads[i : i + 1] for i in range(heads.shape[0])], axis=1)
    flat = jnp.broadcast_to(flat, (8, flat.shape[1])).astype(BF16)
    terms = jnp.dot(flat, proj_ref[...], preferred_element_type=F32)
    tile = jnp.concatenate(
        [terms[0:1, i * LANES : (i + 1) * LANES] for i in range(out_ref.shape[1])], axis=0
    )
    out_ref[...] = jnp.broadcast_to(tile[None], out_ref.shape)


def residual_body(
    parts_ref, hidden_ref, attn_gain_ref, ffw_gain_ref, residual_ref, all_ref
):
    attn = jnp.sum(parts_ref[...], axis=0)
    width = attn.shape[0] * attn.shape[1]
    residual = (
        hidden_ref[...].astype(F32)
        + attn * inv_rms(tile_sum(attn * attn), width) * attn_gain_ref[...]
    )
    residual_ref[...] = residual
    ffw_in = residual * inv_rms(tile_sum(residual * residual), width) * ffw_gain_ref[...]
    all_ref[...] = jnp.broadcast_to(ffw_in.astype(BF16)[None], all_ref.shape)


def ffw_body(x_ref, gate_ref, up_ref, down_ref, out_ref):
    x = x_ref[...]
    across = (((1,), (1,)), ((), ()))
    gate = lax.dot_general(x, gate_ref[...], across, preferred_element_type=F32)
    up = lax.dot_general(x, up_ref[...], across, preferred_element_type=F32)
    units = (jax.nn.gelu(gate, approximate=True) * up).astype(BF16)
    out_ref[...] = jnp.dot(units, down_ref[...], preferred_element_type=F32).astype(BF16)


def output_body(terms_ref, residual_ref, gain_ref, all_ref):
    total = jnp.sum(terms_ref[...].astype(F32), axis=0)
    width = total.shape[0] * total.shape[1]
    row = residual_ref[...] + total * inv_rms(tile_sum(total * total), width) * gain_ref[...]
    all_ref[...] = jnp.broadcast_to(row.astype(BF16)[None], all_ref.shape)


def gather_body(source_ref, pages_ref, *outs):
    per = outs[0].shape[0]
    slots = pages_ref.shape[0]
    for j, out in enumerate(outs):

        @pl.loop(0, per, unroll=4)
        def _(q, j=j, out=out):
            source = source_ref[j * per + q]
            page = pages_ref[jnp.minimum(source, slots - 1)]
            out[q] = jnp.where(source < slots, page, jnp.zeros_like(page))


def regroup_body(count, *refs):
    ins, outs = refs[:count], refs[count:-3]
    held, in_sem, out_sem = refs[-3:]
    cap = outs[0].shape[0] // count
    for j in range(len(outs)):
        for i, chunk in enumerate(ins):
            pltpu.make_async_copy(
                chunk.at[j * cap : (j + 1) * cap], held.at[j, i * cap : (i + 1) * cap], in_sem.at[j]
            ).start()
    for j, out in enumerate(outs):
        pltpu.make_async_copy(out, held.at[j], in_sem.at[j]).wait()
        pltpu.make_async_copy(held.at[j], out, out_sem.at[j]).start()
    for j, out in enumerate(outs):
        pltpu.make_async_copy(held.at[j], out, out_sem.at[j]).wait()


def place_body(cap, tile, place_ref, arrive_ref, fresh_ref, *refs):
    chunks, out = refs[:-4], refs[-4]
    held, in_sem, out_sem = refs[-3:]
    page = out.shape[1]
    inner = chunks[0].shape[0] // cap
    for j, chunk in enumerate(chunks):
        for i in range(inner):
            at = place_ref[j * inner + i] * cap
            pltpu.make_async_copy(
                chunk.at[i * cap : (i + 1) * cap], held.at[pl.ds(at, cap)], in_sem
            ).start()
    pltpu.make_async_copy(out, held, in_sem).wait()

    @pl.loop(0, fresh_ref.shape[0])
    def _(r):
        where = arrive_ref[r]

        @pl.when(where >= 0)
        def _():
            new = fresh_ref[r].astype(F32)
            row = jnp.concatenate([new[tile : tile + 1], new[tile + 1 : tile + 2]], axis=1)
            old = held[where // page].astype(F32)
            here = lax.broadcasted_iota(jnp.int32, old.shape, 0) == where % page
            held[where // page] = jnp.where(here, row, old).astype(BF16)

    copy = pltpu.make_async_copy(held, out, out_sem)
    copy.start()
    copy.wait()


def local(
    hidden,
    positions,
    cache_len,
    page_table,
    move_dest,
    paged_keys,
    paged_values,
    qkv_projection,
    query_norm_gain,
    key_gain,
    output_proj,
    input_gain,
    attn_gain,
    ffw_gain,
    final_gain,
    gate_weight,
    up_weight,
    down_weight,
):
    blocks = lax.axis_size("blk")
    kv_size = lax.axis_size("kv")
    device = lax.axis_index("blk")
    requests, model = hidden.shape
    head = query_norm_gain.shape[0]
    slots, page, _ = paged_keys.shape
    pages_per_seq = page_table.shape[1]
    capacity = max(2, (slots + blocks - 1) // blocks)
    recv_slots = blocks * capacity
    feature_rows, columns = qkv_projection.shape
    groups = columns // head - 2
    col_tiles = columns // LANES
    model_tiles = model // LANES
    assert requests == blocks

    hidden32 = hidden.astype(F32)
    scale = lax.rsqrt(jnp.mean(hidden32 * hidden32, axis=-1, keepdims=True) + EPSILON)
    start = device * feature_rows
    normed = (
        lax.dynamic_slice_in_dim(hidden, start, feature_rows, 1).astype(F32)
        * scale
        * lax.dynamic_slice_in_dim(input_gain, start, feature_rows, 0)
    ).astype(BF16)
    terms = jnp.dot(normed, qkv_projection, preferred_element_type=F32).astype(BF16)
    terms = exchange(terms.reshape(requests, col_tiles, LANES))

    cores, depth = 2, 8
    near = blocks // depth
    across = device // (depth * cores)
    along = device // cores % depth
    core = device % cores

    def index(x, z, c):
        return (x % (near // cores) * depth + z % depth) * cores + c

    def pairs(step_near, step_along):
        out = []
        for b in range(blocks):
            x, z, c = b // (depth * cores), b // cores % depth, b % cores
            out.append(
                (b, index(x + step_near // cores, z + step_along, c ^ (step_near % cores)))
            )
        return out

    to_near = [pairs(k, 0) for k in range(near)]
    to_along = [pairs(0, k) for k in range(depth)]

    vmem = pl.BlockSpec(memory_space=pltpu.VMEM)
    smem = pl.BlockSpec(memory_space=pltpu.SMEM)
    anywhere = pl.BlockSpec(memory_space=pl.ANY)

    def buffers(count):
        return [jax.ShapeDtypeStruct((recv_slots // count, page, head), BF16)] * count

    def gather(pages, order, count):
        match = order[None, :] == jnp.arange(recv_slots, dtype=jnp.int32)[:, None]
        source_of = slots + jnp.sum(jnp.where(match, slot_iota[None, :] - slots, 0), axis=1)
        return pl.pallas_call(
            gather_body,
            out_shape=buffers(count),
            in_specs=[smem, vmem],
            out_specs=[vmem] * count,
            cost_estimate=pl.CostEstimate(
                flops=0, bytes_accessed=6 * slots * page * head, transcendentals=0
            ),
        )(source_of, pages)

    def regroup(chunks, count):
        return pl.pallas_call(
            functools.partial(regroup_body, len(chunks)),
            out_shape=buffers(count),
            in_specs=[anywhere] * len(chunks),
            out_specs=[anywhere] * count,
            scratch_shapes=[
                pltpu.VMEM((count, recv_slots // count, page, head), BF16),
                pltpu.SemaphoreType.DMA((count,)),
                pltpu.SemaphoreType.DMA((count,)),
            ],
            cost_estimate=pl.CostEstimate(
                flops=0, bytes_accessed=8 * slots * page * head, transcendentals=0
            ),
        )(*chunks)

    dest = lax.dynamic_slice_in_dim(move_dest[:, 0], device * slots, slots)
    slot_iota = jnp.arange(slots, dtype=jnp.int32)
    earlier = (dest[None, :] == dest[:, None]) & (slot_iota[None, :] < slot_iota[:, None])
    rank = jnp.sum(earlier.astype(jnp.int32), axis=1)
    step_near = (dest // (depth * cores) - across) % (near // cores) * cores + (dest % cores ^ core)
    step_along = (dest // cores - along) % depth
    keys_sends = gather(paged_keys, (step_near * depth + step_along) * capacity + rank, near)
    values_sends = gather(paged_values, (step_along * near + step_near) * capacity + rank, depth)
    terms, keys_sends, values_sends = tie(terms, keys_sends, values_sends)

    def permutes(sends, targets):
        return [sends[0]] + [
            lax.ppermute(sends[k], "blk", targets[k]) for k in range(1, len(sends))
        ]

    def due(value, *wanted):
        done = tie(value, *[moves[k] for moves, steps in wanted for k in steps])
        rest = iter(done[1:])
        for moves, steps in wanted:
            for k in steps:
                moves[k] = next(rest)
        return done[0]

    frequency = jnp.exp(-(2.0 * jnp.arange(head // 2, dtype=F32) / head) * ROPE_LOG)
    position = lax.dynamic_slice_in_dim(positions, device, 1).astype(F32)
    angles = position[:, None] * frequency[None, :]
    tile = (head // LANES, LANES)
    every, own = call(
        head_body,
        (
            jax.ShapeDtypeStruct((requests, col_tiles, LANES), BF16),
            jax.ShapeDtypeStruct((col_tiles, LANES), BF16),
        ),
        5,
        requests * columns,
        4 * requests * columns,
    )(
        terms,
        jnp.cos(angles),
        jnp.sin(angles),
        query_norm_gain.reshape(tile),
        key_gain.reshape(tile),
    )
    every, *sends = tie(every, *keys_sends, *values_sends)
    keys_first = permutes(sends[:near], to_near)
    values_first = permutes(sends[near:], to_along)
    every = exchange(every)

    slot_ids = device * slots + jnp.arange(slots, dtype=jnp.int32)
    page_starts = jnp.arange(pages_per_seq, dtype=jnp.int32) * page
    held = jnp.clip(cache_len[:, None] - page_starts[None, :], 0, page)
    limit = jnp.sum(
        jnp.where(page_table[:, None, :] == slot_ids[None, :, None], held[:, None, :], 0), axis=-1
    ).astype(BF16)
    parts = call(
        functools.partial(attend_body, groups),
        jax.ShapeDtypeStruct((requests, columns), BF16),
        4,
        4 * groups * requests * slots * page * head,
        4 * slots * page * head,
    )(every.reshape(requests, columns), paged_keys, paged_values, limit)
    parts = exchange(parts.reshape(requests, col_tiles, LANES))
    parts = due(parts, (values_first, (3, 5)), (keys_first, (2, 6, 4)))
    attn_terms = call(
        functools.partial(merge_body, groups),
        jax.ShapeDtypeStruct((kv_size, model_tiles, LANES), F32),
        3,
        16 * groups * head * model,
        2 * groups * head * model,
    )(parts, own, output_proj)

    attn_terms = lax.all_to_all(attn_terms, "kv", split_axis=0, concat_axis=0, tiled=True)
    attn_terms = due(attn_terms, (values_first, (1, 7, 4)), (keys_first, (3, 7)))
    wide = (model_tiles, LANES)
    residual, ffw_in = call(
        residual_body,
        (
            jax.ShapeDtypeStruct(wide, F32),
            jax.ShapeDtypeStruct((requests,) + wide, BF16),
        ),
        4,
        model * 16,
        2 * requests * model,
    )(
        attn_terms,
        lax.dynamic_slice_in_dim(hidden, device, 1, 0).reshape(wide),
        attn_gain.reshape(wide),
        ffw_gain.reshape(wide),
    )
    ffw_in = exchange(ffw_in).reshape(requests, model)
    ffw_in = due(ffw_in, (values_first, (2, 6)), (keys_first, (5, 1)))
    units = gate_weight.shape[1]
    ffw_terms = call(
        ffw_body,
        jax.ShapeDtypeStruct((requests, model), BF16),
        4,
        6 * requests * units * model,
        6 * units * model,
    )(ffw_in, gate_weight.T, up_weight.T, down_weight)
    ffw_terms, *arrived = tie(ffw_terms, *keys_first, *values_first)
    keys_sends = regroup(arrived[:near], depth)
    keys_second = permutes(keys_sends, to_along)
    _, *arrived = tie(keys_sends[0], *arrived[near:])
    values_second = permutes(regroup(arrived, near), to_near)
    ffw_terms = exchange(ffw_terms.reshape((requests,) + wide))
    out_rows = call(
        output_body,
        jax.ShapeDtypeStruct((requests,) + wide, BF16),
        3,
        requests * model,
        4 * requests * model,
    )(ffw_terms, residual, final_gain.reshape(wide))
    out_hidden = exchange(out_rows).reshape(requests, model).astype(F32)

    target = jnp.sum(
        jnp.where(
            jnp.arange(pages_per_seq, dtype=jnp.int32)[None, :] == cache_len[:, None] // page,
            page_table,
            0,
        ),
        axis=1,
    )
    all_dest = move_dest[:, 0]
    all_slots = jnp.arange(all_dest.shape[0], dtype=jnp.int32)
    target_dest = jnp.sum(
        jnp.where(all_slots[None, :] == target[:, None], all_dest[None, :], 0), axis=1
    )
    target_rank = jnp.sum(
        (
            (all_slots[None, :] // slots == target[:, None] // slots)
            & (all_slots[None, :] < target[:, None])
            & (all_dest[None, :] == target_dest[:, None])
        ).astype(jnp.int32),
        axis=1,
    )
    arrival = target // slots * capacity + target_rank
    arrive = jnp.where(target_dest == device, arrival * page + cache_len % page, -1)
    back_along = jnp.arange(depth, dtype=jnp.int32)
    back_near = jnp.arange(near, dtype=jnp.int32)

    def source_index(along_step, near_step):
        return index(
            across - near_step // cores, along - along_step, core ^ (near_step % cores)
        ).reshape(-1)

    def place(chunks, places, tile):
        return pl.pallas_call(
            functools.partial(place_body, capacity, tile),
            out_shape=jax.ShapeDtypeStruct((recv_slots, page, head), BF16),
            in_specs=[smem, smem, vmem] + [anywhere] * len(chunks),
            out_specs=anywhere,
            scratch_shapes=[
                pltpu.VMEM((recv_slots, page, head), BF16),
                pltpu.SemaphoreType.DMA,
                pltpu.SemaphoreType.DMA,
            ],
            cost_estimate=pl.CostEstimate(
                flops=0, bytes_accessed=8 * slots * page * head, transcendentals=0
            ),
        )(places, arrive, every, *chunks)

    by_along = (0, 3, 5, 4, 2, 6, 1, 7)
    by_near = (0, 4, 5, 2, 6, 3, 7, 1)
    relocated_keys = place(
        [keys_second[k] for k in by_along],
        source_index(jnp.array(by_along, jnp.int32)[:, None], back_near[None, :]),
        2 * groups,
    )
    relocated_keys, *values_second = tie(relocated_keys, *values_second)
    relocated_values = place(
        [values_second[k] for k in by_near],
        source_index(back_along[None, :], jnp.array(by_near, jnp.int32)[:, None]),
        2 * groups + 2,
    )
    return (out_hidden, relocated_keys, relocated_values)


def solution(mesh):
    return jax.shard_map(
        local,
        mesh=mesh,
        in_specs=(
            P(),
            P(),
            P(),
            P(),
            P(),
            P("blk", None, "kv"),
            P("blk", None, "kv"),
            P("blk", "kv"),
            P(),
            P(),
            P("kv", None),
            P(),
            P(),
            P(),
            P(),
            P(None, "blk"),
            P(None, "blk"),
            P("blk", None),
        ),
        out_specs=(P(), P("blk", None, "kv"), P("blk", None, "kv")),
        check_vma=False,
    )
```
